256 devices in a mesh: mesh: 32 (over x, y, core), elec: 8 (over z).
Axes of the slice: x: 4, y: 4, z: 8, core: 2. Of those that a mesh axis runs over, the one named last changes fastest.
Arguments:
- rhs: float32 [65536, 1024], P('mesh', 'elec'), may hold values from -18 to 18, as said below
- diagonal: float32 [65536], P('mesh'), may hold values from 1 to 3
- tile_values: bfloat16 [2048, 128, 128], P('mesh'), may hold values from -0.011875 to 0.011875
- tile_rows: int32 [2048], P('mesh'), may hold values from 0 to 15
- tile_offsets: int32 [2048], P('mesh'), may hold values from 0 to 2
- tile_count: int32 [32], P('mesh'), may hold values from 1 to 64, 1280 in all
- node_count: int32 [32], P('mesh'), may hold values from 1 to 2048, 49152 in all
- inc_values: bfloat16 [512, 128, 128], P('mesh'), may hold values from -0.1875 to 0.1875
- inc_rows: int32 [512], P('mesh'), may hold values from 0 to 15
- inc_blocks: int32 [512], P('mesh'), may hold values from 0 to 63
Outputs:
- solution: float32 [65536, 1024], P('mesh', 'elec')
- lead_field: float32 [8192, 1024], P(('mesh', 'elec'))
The draws below stay inside these ranges and needn't reach their ends.
Inputs may be any that keep to these rules, and one draw needn't show every extreme that they name: `rhs`: Right-hand sides of one partition share a scale.
All inputs are finite; a program needn't handle non-finite values. No bound on the sum of `tile_count` or of `node_count` on one device may be relied on, other than what follows from the above.
Results may differ from the reference program's by a relative error of at most 0.0003.
Values sent between devices are 32-bit elements; how exact they have to be, the bound alone decides.
No kernel may reach another device: no remote copies, remote signals or barrier semaphores. Data moves between devices by JAX's collectives and lax.ppermute only.
A program may use at most 64 MiB of HBM per device.

```python
import math
import jax
import jax.numpy as jnp
import numpy as np
from jax import lax

BLK = 128
ECOL = 128
ROWB_DEV = 16
HB = 2
SRCB_DEV = 2
ITERS = 2
NODES_DEV = 2048
NODES = 65536
TILES_DEV = 64
TILES = 2048
INC_DEV = 16
COLS = 1024
SRCB = 64
SOURCES = 8192
N_MESH = 32
N_ELEC = 8


def group_mixing(key):
    vectors = jax.random.normal(key, (2, N_ELEC, ECOL, ECOL), jnp.float32)
    identity = jnp.broadcast_to(jnp.eye(ECOL, dtype=jnp.float32), (2, N_ELEC, ECOL, ECOL))

    def reflect(turn, frames):
        vector = lax.dynamic_index_in_dim(vectors, turn, 2, keepdims=False)
        projected = jnp.einsum('agij,agj->agi', frames, vector, precision=lax.Precision.HIGHEST)
        lengths = jnp.sum(vector * vector, -1)
        return frames - 2.0 * projected[:, :, :, None] * vector[:, :, None, :] / lengths[:, :, None, None]
    frames = lax.fori_loop(0, ECOL, reflect, identity)
    singular = 10.0 ** (jnp.arange(ECOL).astype(jnp.float32) / max(ECOL - 1, 1))
    singular = singular / jnp.sqrt(jnp.mean(singular * singular))
    return jnp.einsum('gij,j,gkj->gik', frames[0], singular, frames[1], precision=lax.Precision.HIGHEST)


def mix_columns(values, mixing):
    grouped = values.reshape(NODES, N_ELEC, ECOL)
    return jnp.einsum('ngi,gik->ngk', grouped, mixing, precision=lax.Precision.HIGHEST).reshape(NODES, COLS)


def draw_rhs(key, part):
    node_rows = jnp.arange(NODES)
    parts_all = NODES // NODES_DEV
    portion = (node_rows // NODES_DEV).astype(jnp.float32) / max(parts_all - 1, 1)
    mixing = group_mixing(jax.random.fold_in(key, 11))
    row_scale = 3.0 ** portion
    noise = jax.random.normal(key, (NODES, COLS), jnp.float32)
    mixed = mix_columns(noise, mixing)
    return jnp.clip(mixed, -6.0, 6.0) * row_scale[:, None]


def draw_tile_values(key, part):
    sigma = 0.15 / math.sqrt(8.0 * BLK)
    return (jnp.clip(jax.random.normal(key, (TILES, BLK, BLK), jnp.float32), -2.5, 2.5) * sigma).astype(jnp.bfloat16)


def place_ends(array, key, smallest, high):
    dims = array.shape
    place = [jax.random.randint(jax.random.fold_in(key, axis), (), 0, dims[axis]) for axis in range(len(dims))]
    array = array.at[tuple(place)].set(smallest)
    longest = dims.index(max(dims))
    place[longest] = (place[longest] + 1) % dims[longest]
    return array.at[tuple(place)].set(high)


def levels(own_key, extent, shards, low, high):
    def one(axis_at, blocks):
        steps = jax.random.uniform(jax.random.fold_in(jax.random.fold_in(own_key, 6), axis_at), (blocks,), jnp.float32, low / len(shards), high / len(shards))
        return jnp.repeat(jnp.exp(steps), extent[axis_at] // blocks).reshape((-1,) + (1,) * (len(extent) - axis_at - 1))

    loudness = one(*shards[0])
    for cut in shards[1:]:
        loudness = loudness * one(*cut)
    return loudness


def profile(count, total, limit, skew):
    portions = [(1 << 20) // math.isqrt(standing ** skew) + 1 for standing in range(2, count + 1)]
    surplus, given = total - limit - (count - 1), [1] * (count - 1)
    while surplus > 0:
        movable = [i for i in range(count - 1) if given[i] < limit]
        whole, budget = sum([portions[i] for i in movable]), surplus
        for i in movable:
            addition = min(limit - given[i], max(1, budget * portions[i] // whole), surplus)
            given[i] = given[i] + addition
            surplus = surplus - addition
    return np.array([limit] + given)


def ragged(own_key, amount, total, limit, lean):
    if amount == 2:
        one = jax.random.randint(own_key, (), max(1, total - limit), min(limit, total - 1) + 1)
        return jnp.stack([one, total - one])
    sizes = jnp.asarray(profile(amount, total, limit, lean), jnp.int32)
    couples = (amount - 1) // 2
    giver, receiver = sizes[1:1 + 2 * couples:2], sizes[2:2 + 2 * couples:2]
    room = jnp.minimum(giver - 1, limit - receiver)
    shifted = jax.random.randint(jax.random.fold_in(own_key, 1), (couples,), 0, 1 << 20) % (room + 1)
    sizes = sizes.at[1:1 + 2 * couples:2].set(giver - shifted).at[2:2 + 2 * couples:2].set(receiver + shifted)
    return sizes[jax.random.permutation(jax.random.fold_in(own_key, 2), amount)]


def normal_values(key, shape, scale, most, cuts=(), kind=jnp.bfloat16):
    loudness = levels(key, shape, cuts, -0.22, 0.18) if cuts else 1.0
    array = jax.random.normal(key, shape, jnp.float32) * scale * loudness
    return jnp.minimum(jnp.maximum(array, -most), most).astype(kind)


def setup_inputs(seed: int = 0) -> dict:
    keys = jax.random.split(jax.random.key(seed), 11)
    return {
        "rhs": draw_rhs(jax.random.fold_in(keys[10], 71), 0),
        "diagonal": jnp.clip(jnp.exp(math.log(3.0) - 1.0986123 * jax.random.uniform(keys[1], (NODES,), jnp.float32) ** levels(keys[1], (NODES,), ((0, 32),), -0.2, 0.2)), 1.0, 3.0),
        "tile_values": draw_tile_values(jax.random.fold_in(keys[10], 71), 0),
        "tile_rows": place_ends(jax.random.randint(keys[3], (TILES,), 0, ROWB_DEV), jax.random.fold_in(keys[3], 1), 0, ROWB_DEV - 1).astype(jnp.int32),
        "tile_offsets": place_ends(jax.random.randint(keys[4], (TILES,), 0, HB + 1), jax.random.fold_in(keys[4], 1), 0, HB).astype(jnp.int32),
        "tile_count": ragged(keys[5], N_MESH, N_MESH * TILES_DEV * 5 // 8, TILES_DEV, 1).astype(jnp.int32),
        "node_count": ragged(keys[6], N_MESH, N_MESH * NODES_DEV * 3 // 4, NODES_DEV, 1).astype(jnp.int32),
        "inc_values": normal_values(keys[7], (N_MESH * INC_DEV, BLK, BLK), (BLK * INC_DEV // SRCB_DEV) ** -0.5, 0.1875, ((0, 32),)),
        "inc_rows": place_ends(jax.random.randint(keys[8], (N_MESH * INC_DEV,), 0, ROWB_DEV), jax.random.fold_in(keys[8], 1), 0, ROWB_DEV - 1).astype(jnp.int32),
        "inc_blocks": place_ends(jax.random.randint(keys[9], (N_MESH * INC_DEV,), 0, SRCB), jax.random.fold_in(keys[9], 1), 0, SRCB - 1).astype(jnp.int32),
    }


def reference(rhs, diagonal, tile_values, tile_rows, tile_offsets, tile_count, node_count, inc_values, inc_rows, inc_blocks):
    highest = lax.Precision.HIGHEST
    nblocks = N_MESH * ROWB_DEV
    index = jnp.arange(NODES)
    owner = index // NODES_DEV
    mask = (index % NODES_DEV < node_count[owner]).astype(jnp.float32)

    def operate(field):
        width = field.shape[1]
        blocks = field.reshape(nblocks, BLK, width)
        padded = jnp.concatenate([blocks, jnp.zeros((HB, BLK, width), jnp.float32)], 0)

        def one_part(part, total):
            start = part * TILES_DEV
            coupling = lax.dynamic_slice_in_dim(tile_values, start, TILES_DEV, 0).astype(jnp.float32)
            live = (jnp.arange(TILES_DEV) < tile_count[part]).astype(jnp.float32)
            coupling = coupling * live[:, None, None]
            row_block = part * ROWB_DEV + lax.dynamic_slice_in_dim(tile_rows, start, TILES_DEV, 0)
            col_block = row_block + lax.dynamic_slice_in_dim(tile_offsets, start, TILES_DEV, 0)
            forward = jnp.einsum('tij,tjc->tic', coupling, padded[col_block], precision=highest)
            backward = jnp.einsum('tji,tjc->tic', coupling, padded[row_block], precision=highest)
            return total.at[row_block].add(forward).at[col_block].add(backward)
        summed = lax.fori_loop(0, N_MESH, one_part, jnp.zeros_like(padded))
        return mask[:, None] * (diagonal[:, None] * field + summed[:nblocks].reshape(NODES, width))

    def gram(left, right):
        return jnp.einsum('ngi,ngj->gij', left.reshape(NODES, N_ELEC, ECOL), right.reshape(NODES, N_ELEC, ECOL), precision=highest)

    def apply_right(field, matrix):
        return jnp.einsum('ngi,gij->ngj', field.reshape(NODES, N_ELEC, ECOL), matrix, precision=highest).reshape(NODES, COLS)

    def one_solve(gmat, hmat):
        return jax.scipy.linalg.cho_solve((jnp.linalg.cholesky(gmat), True), hmat)
    solve = jax.vmap(one_solve)
    source = mask[:, None] * rhs
    solution = jnp.zeros((NODES, COLS), jnp.float32)
    residual = source
    direction = source
    norm_now = gram(residual, residual)
    for step in range(ITERS):
        image = operate(direction)
        alpha = solve(gram(direction, image), norm_now)
        solution = solution + apply_right(direction, alpha)
        if step + 1 < ITERS:
            residual = residual - apply_right(image, alpha)
            norm_next = gram(residual, residual)
            beta = solve(norm_now, norm_next)
            direction = residual + apply_right(direction, beta)
            norm_now = norm_next
    sol_blocks = solution.reshape(nblocks, BLK, COLS)

    def lead_part(part, total):
        start = part * INC_DEV
        incidence = lax.dynamic_slice_in_dim(inc_values, start, INC_DEV, 0).astype(jnp.float32)
        row_block = part * ROWB_DEV + lax.dynamic_slice_in_dim(inc_rows, start, INC_DEV, 0)
        target = lax.dynamic_slice_in_dim(inc_blocks, start, INC_DEV, 0)
        contrib = jnp.einsum('tns,tnc->tsc', incidence, sol_blocks[row_block], precision=highest)
        return total.at[target].add(contrib)
    lead = lax.fori_loop(0, N_MESH, lead_part, jnp.zeros((SRCB, BLK, COLS), jnp.float32))
    return (solution, lead.reshape(SOURCES, COLS))
```

```python
import functools

import jax
import jax.numpy as jnp
from jax import lax
from jax.experimental import pallas as pl
from jax.experimental.pallas import tpu as pltpu
from jax.sharding import PartitionSpec as P

HB = 2
SRCB_DEV = 2
BLK = 128
SHIFT = 2.0
F32 = jnp.float32
BF16 = jnp.bfloat16
HIGHEST = lax.Precision.HIGHEST


def mm(left, right, dims=((1,), (0,))):
    return lax.dot_general(left, right, (dims, ((), ())), preferred_element_type=F32)


def mmh(left, right, dims=((1,), (0,))):
    return lax.dot_general(
        left, right, (dims, ((), ())), preferred_element_type=F32, precision=HIGHEST
    )


def split(value):
    high = value.astype(BF16)
    return high, (value - high.astype(F32)).astype(BF16)


def rows_of(block):
    return block * BLK + lax.broadcasted_iota(jnp.int32, (BLK, BLK), 0)


def column(line):
    return jnp.transpose(jnp.broadcast_to(line, (BLK, BLK)))


def tile_loop(count, unroll, one):
    def group(g, carry):
        for k in range(unroll):
            one(g * unroll + k)
        return carry

    lax.fori_loop(0, count // unroll, group, 0)

    def rest(t, carry):
        one(t)
        return carry

    lax.fori_loop(count // unroll * unroll, count, rest, 0)


def first_kernel(
    trow, toff, tcount, ncount, rhs, diag, tiles, field, part, ahead, behind, acc, pieces
):
    rowb = rhs.shape[0] // BLK
    live = ncount[0]

    def prepare(b, carry):
        at = pl.ds(pl.multiple_of(b * BLK, BLK), BLK)
        value = jnp.where(rows_of(b) < live, rhs[at, :], 0.0)
        field[at, :] = value
        high, low = split(value)
        pieces[b, :BLK, :] = high
        pieces[b, BLK:, :] = low
        acc[b] = (column(diag[pl.ds(b, 1), :]) - SHIFT) * value
        return carry

    lax.fori_loop(0, rowb, prepare, 0)
    for b in range(rowb, rowb + HB):
        acc[b] = jnp.zeros((BLK, BLK), F32)
        pieces[b] = jnp.zeros((2 * BLK, BLK), BF16)

    def one(t):
        r = trow[t]
        c = r + toff[t]
        tile = tiles[t]
        flipped = jnp.transpose(tile)
        forward = mm(jnp.concatenate([tile, tile], 1), pieces[c])
        backward = mm(jnp.concatenate([flipped, flipped], 1), pieces[r])
        acc[r] += forward
        acc[c] += backward

    tile_loop(tcount[0], 4, one)

    def finish(b, carry):
        at = pl.ds(pl.multiple_of(b * BLK, BLK), BLK)
        part[at, :] = jnp.where(rows_of(b) < live, acc[b], 0.0)
        return carry

    lax.fori_loop(0, rowb, finish, 0)
    head = HB * BLK
    ahead[:head, :] = field[:head, :]
    ahead[head : 2 * head, :] = part[:head, :]
    ahead[2 * head :, :] = jnp.full((8, BLK), live.astype(F32))
    for b in range(HB):
        behind[b * BLK : (b + 1) * BLK, :] = acc[rowb + b]


def pack(first, second):
    i = lax.broadcasted_iota(jnp.int32, (BLK, BLK), 0)
    j = lax.broadcasted_iota(jnp.int32, (BLK, BLK), 1)
    line = jnp.sum(jnp.where(i == j, second, 0.0), 0, keepdims=True)
    return jnp.where(i <= j, first, second), line


def unpack(packed, line):
    i = lax.broadcasted_iota(jnp.int32, (BLK, BLK), 0)
    j = lax.broadcasted_iota(jnp.int32, (BLK, BLK), 1)
    flipped = jnp.transpose(packed)
    first = jnp.where(i <= j, packed, flipped)
    second = jnp.where(i > j, packed, flipped)
    return first, jnp.where(i == j, jnp.broadcast_to(line, (BLK, BLK)), second)


def second_kernel(
    trow, toff, tcount, ncount, core,
    field, part, diag, tiles, behind, from_behind, from_ahead,
    image, keep, give, acc, pieces, wide_h, wide_l, u_h, u_l,
):
    rowb = field.shape[0] // BLK
    live = ncount[0]
    count = tcount[0]
    head = HB * BLK
    edge = rowb - HB

    for b in range(HB):
        high, low = split(from_ahead[b * BLK : (b + 1) * BLK, :])
        pieces[rowb + b, :BLK, :] = high
        pieces[rowb + b, BLK:, :] = low
        acc[edge + b] = jnp.zeros((BLK, BLK), F32)

    def reach(t, carry):
        r = trow[t]
        c = r + toff[t]

        @pl.when(c >= rowb)
        def _():
            tile = tiles[t]
            acc[r] += mm(jnp.concatenate([tile, tile], 1), pieces[c])

        return carry

    lax.fori_loop(0, count, reach, 0)

    count_ahead = from_ahead[2 * head : 2 * head + 1, :]
    for b in range(HB):
        at = slice(b * BLK, (b + 1) * BLK)
        row = rows_of(b).astype(F32)
        value = from_ahead[head + b * BLK : head + (b + 1) * BLK, :]
        value = value + jnp.where(row < count_ahead, behind[at, :], 0.0)
        high, low = split(value)
        pieces[rowb + b, :BLK, :] = high
        pieces[rowb + b, BLK:, :] = low

    def settle(b, extra):
        at = pl.ds(pl.multiple_of(b * BLK, BLK), BLK)
        value = part[at, :]
        if extra is not None:
            value = value + jnp.where(rows_of(b) < live, extra, 0.0)
        image[at, :] = value
        high, low = split(value)
        pieces[b, :BLK, :] = high
        pieces[b, BLK:, :] = low
        wide_h[at, BLK:] = high
        wide_l[at, BLK:] = low
        high, low = split(field[at, :])
        wide_h[at, :BLK] = high
        wide_l[at, :BLK] = low
        acc[b] = (0.5 * (column(diag[pl.ds(b, 1), :]) - SHIFT)) * value

    for b in range(HB):
        settle(b, from_behind[b * BLK : (b + 1) * BLK, :])
    for b in range(edge, rowb):
        settle(b, acc[b])

    def middle(b, carry):
        settle(b, None)
        return carry

    lax.fori_loop(HB, edge, middle, 0)

    def one(t):
        r = trow[t]
        tile = tiles[t]
        acc[r] += mm(jnp.concatenate([tile, tile], 1), pieces[r + toff[t]])

    tile_loop(count, 4, one)

    def widen(b, carry):
        at = pl.ds(pl.multiple_of(b * BLK, BLK), BLK)
        high, low = split(acc[b])
        u_h[at, :] = high
        u_l[at, :] = low
        return carry

    lax.fori_loop(0, rowb, widen, 0)

    first = ((0,), (0,))
    straight = mm(wide_h[...], wide_h[...], first)
    cross = mm(wide_h[...], wide_l[...], first)
    n0 = straight[:BLK, :BLK] + cross[:BLK, :BLK] + jnp.transpose(cross[:BLK, :BLK])
    n1 = straight[:BLK, BLK:] + cross[:BLK, BLK:] + jnp.transpose(cross[BLK:, :BLK])
    n2 = straight[BLK:, BLK:] + cross[BLK:, BLK:] + jnp.transpose(cross[BLK:, BLK:])
    half = mm(wide_h[:, BLK:], u_h[...], first)
    half = half + mm(wide_h[:, BLK:], u_l[...], first) + mm(wide_l[:, BLK:], u_h[...], first)
    n3 = half + jnp.transpose(half)
    n1 = 0.5 * (n1 + jnp.transpose(n1))
    low_packed, low_line = pack(n0, n1)
    high_packed, high_line = pack(n2, n3)

    def place(low_ref, high_ref):
        low_ref[:BLK, :] = low_packed
        low_ref[BLK:, :] = jnp.broadcast_to(low_line, (8, BLK))
        high_ref[:BLK, :] = high_packed
        high_ref[BLK:, :] = jnp.broadcast_to(high_line, (8, BLK))

    @pl.when(core[0] == 0)
    def _():
        place(keep, give)

    @pl.when(core[0] != 0)
    def _():
        place(give, keep)


def invert(matrix):
    n = matrix.shape[0]
    step = 8
    lane = lax.broadcasted_iota(jnp.int32, (step, n), 1)
    sub = lax.broadcasted_iota(jnp.int32, (step, n), 0)
    for k in range(n // step):
        base = k * step
        panel = matrix[base : base + step, :]
        inside = (lane >= base) & (lane < base + step)
        unit = (lane - base == sub).astype(F32)
        work, extra = panel, unit
        for j in range(step):
            factor = work[:, base + j : base + j + 1]
            scale = 1.0 / factor[j : j + 1, :]
            row = work[j : j + 1, :] * scale
            other = extra[j : j + 1, :] * scale
            here = sub == j
            work = jnp.where(here, row, work - factor * row)
            extra = jnp.where(here, other, extra - factor * other)
        outer = jnp.where(inside, 0.0, panel)
        rows = jnp.where(inside, -extra, work)
        matrix = jnp.where(inside[:1, :], 0.0, matrix) - mmh(outer, rows, ((0,), (0,)))
        pieces = []
        if base:
            pieces.append(matrix[:base, :])
        pieces.append(rows)
        if base + step < n:
            pieces.append(matrix[base + step :, :])
        matrix = jnp.concatenate(pieces, 0)
    return -matrix


def solve_kernel(core, mine, other, out):
    first = core[0] == 0
    low = jnp.where(first, mine[...], other[...])
    high = jnp.where(first, other[...], mine[...])
    n0, n1 = unpack(low[:BLK, :], low[BLK : BLK + 1, :])
    n2, n3 = unpack(high[:BLK, :], high[BLK : BLK + 1, :])
    m1 = n1 + SHIFT * n0
    m2 = n2 + SHIFT * n1
    m3 = n3 + SHIFT * n2
    inverse = invert(m1)
    both = mmh(inverse, jnp.concatenate([m2, n0], 1))
    across = mmh(m2, both)
    schur = m3 - across[:, :BLK]
    y1 = mmh(invert(schur), n1 - across[:, BLK:])
    y0 = both[:, BLK:] - mmh(both[:, :BLK], y1)
    out[:BLK, :] = y0
    out[BLK:, :] = y1


def third_kernel(irow, iblk, core, field, image, coef, inc, sol, keep, give, pieces):
    rowb = field.shape[0] // BLK
    y0h, y0l = split(coef[:BLK, :])
    y1h, y1l = split(coef[BLK:, :])
    stack_h = jnp.concatenate([y0h, y1h], 0)
    stack_l = jnp.concatenate([y0l, y1l], 0)
    keep[...] = jnp.zeros(keep.shape, F32)
    give[...] = jnp.zeros(give.shape, F32)

    def combine(b, carry):
        at = pl.ds(pl.multiple_of(b * BLK, BLK), BLK)
        fh, fl = split(field[at, :])
        ih, il = split(image[at, :])
        left_h = jnp.concatenate([fh, ih], 1)
        left_l = jnp.concatenate([fl, il], 1)
        value = mm(left_h, stack_h) + (mm(left_h, stack_l) + mm(left_l, stack_h))
        sol[at, :] = value
        high, low = split(value)
        pieces[b, :BLK, :] = high
        pieces[b, BLK:, :] = low
        return carry

    lax.fori_loop(0, rowb, combine, 0)

    def add(u, carry):
        flipped = jnp.transpose(inc[u])
        product = mm(jnp.concatenate([flipped, flipped], 1), pieces[irow[u]])
        block = iblk[u]
        owner = block // SRCB_DEV
        at = owner // 2 * SRCB_DEV + block % SRCB_DEV
        mine = owner % 2 == core[0]

        @pl.when(mine)
        def _():
            keep[at] += product

        @pl.when(jnp.logical_not(mine))
        def _():
            give[at] += product

        return carry

    lax.fori_loop(0, inc.shape[0], add, 0)


def call(kernel, n_scalar, n_vector, outs, scratch=()):
    vmem = pl.BlockSpec(memory_space=pltpu.VMEM)
    smem = pl.BlockSpec(memory_space=pltpu.SMEM)
    return pl.pallas_call(
        kernel,
        in_specs=[smem] * n_scalar + [vmem] * n_vector,
        out_specs=[vmem] * len(outs),
        out_shape=[jax.ShapeDtypeStruct(shape, F32) for shape in outs],
        scratch_shapes=[pltpu.VMEM(shape, dtype) for shape, dtype in scratch],
        compiler_params=pltpu.CompilerParams(vmem_limit_bytes=48 * 1024 * 1024),
    )


def body(
    sides, rhs, diagonal, tile_values, tile_rows, tile_offsets, tile_count, node_count,
    inc_values, inc_rows, inc_blocks,
):
    nx, ny = sides
    nodes, width = rhs.shape
    rowb = nodes // BLK
    head = HB * BLK
    count = 2 * nx * ny
    lead_half = nx * ny * SRCB_DEV
    core = (lax.axis_index("mesh") % 2).astype(jnp.int32)[None]
    diag = diagonal.reshape(rowb, BLK)

    def place(x, y, c):
        return (x % nx * ny + y % ny) * 2 + c

    def moved(value, dx, dy):
        return lax.ppermute(value, "mesh", [
            (place(x, y, c), place(x + dx, y + dy, c))
            for x in range(nx) for y in range(ny) for c in range(2)
        ])

    def swap(value):
        return lax.ppermute(value, "mesh", [(i, i ^ 1) for i in range(count)])

    field, part, ahead, behind = call(
        first_kernel, 4, 3,
        [(nodes, width), (nodes, width), (2 * head + 8, width), (head, width)],
        [((rowb + HB, BLK, BLK), F32), ((rowb + HB, 2 * BLK, BLK), BF16)],
    )(tile_rows, tile_offsets, tile_count, node_count, rhs, diag, tile_values)
    from_ahead = lax.ppermute(ahead, "mesh", [(i + 1, i) for i in range(count - 1)])
    from_behind = lax.ppermute(behind, "mesh", [(i, i + 1) for i in range(count - 1)])
    image, keep, give = call(
        second_kernel, 5, 7,
        [(nodes, width), (BLK + 8, BLK), (BLK + 8, BLK)],
        [
            ((rowb + HB, BLK, BLK), F32), ((rowb + HB, 2 * BLK, BLK), BF16),
            ((nodes, 2 * BLK), BF16), ((nodes, 2 * BLK), BF16),
            ((nodes, BLK), BF16), ((nodes, BLK), BF16),
        ],
    )(tile_rows, tile_offsets, tile_count, node_count, core,
      field, part, diag, tile_values, behind, from_behind, from_ahead)
    total = keep + swap(give)
    total = total + functools.reduce(jnp.add, [moved(total, d, 0) for d in range(1, nx)])
    total = total + functools.reduce(jnp.add, [moved(total, 0, d) for d in range(1, ny)])
    (coef,) = call(solve_kernel, 1, 2, [(2 * BLK, BLK)])(core, total, swap(total))
    solution, keep, give = call(
        third_kernel, 3, 4,
        [(nodes, width), (lead_half, BLK, BLK), (lead_half, BLK, BLK)],
        [((rowb, 2 * BLK, BLK), BF16)],
    )(inc_rows, inc_blocks, core, field, image, coef, inc_values)
    half = (keep + swap(give)).reshape(nx * ny, SRCB_DEV * BLK, width)
    groups = [[2 * i + c for i in range(nx * ny)] for c in range(2)]
    got = lax.all_to_all(
        half, "mesh", split_axis=0, concat_axis=0, tiled=True, axis_index_groups=groups
    )
    lead = lax.all_to_all(got.sum(0), "elec", split_axis=0, concat_axis=1, tiled=True)
    return solution, lead


def solution(mesh):
    placed = (
        P("mesh", "elec"),
        P("mesh"),
        P("mesh", None, None),
        P("mesh"),
        P("mesh"),
        P("mesh"),
        P("mesh"),
        P("mesh", None, None),
        P("mesh"),
        P("mesh"),
    )
    return jax.shard_map(
        functools.partial(body, (4, 4)),
        mesh=mesh,
        in_specs=placed,
        out_specs=(P("mesh", "elec"), P(("mesh", "elec"), None)),
        check_vma=False,
    )
```

```python
import functools

import jax
import jax.numpy as jnp
from jax import lax
from jax.experimental import pallas as pl
from jax.experimental.pallas import tpu as pltpu
from jax.sharding import PartitionSpec as P

HB = 2
SRCB_DEV = 2
BLK = 128
SHIFT = 2.0
F32 = jnp.float32
BF16 = jnp.bfloat16
HIGHEST = lax.Precision.HIGHEST


def mm(left, right, dims=((1,), (0,))):
    return lax.dot_general(left, right, (dims, ((), ())), preferred_element_type=F32)


def mmh(left, right, dims=((1,), (0,))):
    return lax.dot_general(
        left, right, (dims, ((), ())), preferred_element_type=F32, precision=HIGHEST
    )


def split(value):
    high = value.astype(BF16)
    return high, (value - high.astype(F32)).astype(BF16)


def rows_of(block):
    return block * BLK + lax.broadcasted_iota(jnp.int32, (BLK, BLK), 0)


def column(line):
    return jnp.transpose(jnp.broadcast_to(line, (BLK, BLK)))


def tile_loop(count, unroll, one):
    def group(g, carry):
        for k in range(unroll):
            one(g * unroll + k)
        return carry

    lax.fori_loop(0, count // unroll, group, 0)

    def rest(t, carry):
        one(t)
        return carry

    lax.fori_loop(count // unroll * unroll, count, rest, 0)


def fetch(pairs, sems):
    copies = [
        pltpu.make_async_copy(source, target, sems.at[i])
        for i, (source, target) in enumerate(pairs)
    ]
    for copy in copies:
        copy.start()
    return copies


def first_kernel(
    tcount, ncount, trow_far, toff_far, rhs_far, diag_far, tiles_far,
    field, part, ahead, behind, acc, pieces, trow, toff, rhs, diag, tiles, sems,
):
    get_rhs, get_diag, get_row, get_off, get_tiles = fetch(
        [(rhs_far, rhs), (diag_far, diag), (trow_far, trow), (toff_far, toff), (tiles_far, tiles)],
        sems,
    )
    get_rhs.wait()
    get_diag.wait()
    rowb = rhs.shape[0] // BLK
    live = ncount[0]

    def prepare(b, carry):
        at = pl.ds(pl.multiple_of(b * BLK, BLK), BLK)
        value = jnp.where(rows_of(b) < live, rhs[at, :], 0.0)
        field[at, :] = value
        high, low = split(value)
        pieces[b, :BLK, :] = high
        pieces[b, BLK:, :] = low
        acc[b] = (column(diag[pl.ds(b, 1), :]) - SHIFT) * value
        return carry

    lax.fori_loop(0, rowb, prepare, 0)
    for b in range(rowb, rowb + HB):
        acc[b] = jnp.zeros((BLK, BLK), F32)
        pieces[b] = jnp.zeros((2 * BLK, BLK), BF16)
    get_row.wait()
    get_off.wait()
    get_tiles.wait()

    def one(t):
        r = trow[t]
        c = r + toff[t]
        tile = tiles[t]
        flipped = jnp.transpose(tile)
        forward = mm(jnp.concatenate([tile, tile], 1), pieces[c])
        backward = mm(jnp.concatenate([flipped, flipped], 1), pieces[r])
        acc[r] += forward
        acc[c] += backward

    tile_loop(tcount[0], 4, one)

    def finish(b, carry):
        at = pl.ds(pl.multiple_of(b * BLK, BLK), BLK)
        part[at, :] = jnp.where(rows_of(b) < live, acc[b], 0.0)
        return carry

    lax.fori_loop(0, rowb, finish, 0)
    head = HB * BLK
    ahead[:head, :] = field[:head, :]
    ahead[head : 2 * head, :] = part[:head, :]
    ahead[2 * head :, :] = jnp.full((8, BLK), live.astype(F32))
    for b in range(HB):
        behind[b * BLK : (b + 1) * BLK, :] = acc[rowb + b]


def pack(first, second):
    i = lax.broadcasted_iota(jnp.int32, (BLK, BLK), 0)
    j = lax.broadcasted_iota(jnp.int32, (BLK, BLK), 1)
    line = jnp.sum(jnp.where(i == j, second, 0.0), 0, keepdims=True)
    return jnp.where(i <= j, first, second), line


def unpack(packed, line):
    i = lax.broadcasted_iota(jnp.int32, (BLK, BLK), 0)
    j = lax.broadcasted_iota(jnp.int32, (BLK, BLK), 1)
    flipped = jnp.transpose(packed)
    first = jnp.where(i <= j, packed, flipped)
    second = jnp.where(i > j, packed, flipped)
    return first, jnp.where(i == j, jnp.broadcast_to(line, (BLK, BLK)), second)


def second_kernel(
    tcount, ncount, core,
    trow_far, toff_far, diag_far, tiles_far, field, part, behind, from_behind, from_ahead,
    image, keep, give, acc, pieces, wide_h, wide_l, u_h, u_l, trow, toff, diag, tiles, sems,
):
    get_row, get_off, get_diag, get_tiles = fetch(
        [(trow_far, trow), (toff_far, toff), (diag_far, diag), (tiles_far, tiles)], sems
    )
    rowb = field.shape[0] // BLK
    live = ncount[0]
    count = tcount[0]
    head = HB * BLK
    edge = rowb - HB

    for b in range(HB):
        high, low = split(from_ahead[b * BLK : (b + 1) * BLK, :])
        pieces[rowb + b, :BLK, :] = high
        pieces[rowb + b, BLK:, :] = low
        acc[edge + b] = jnp.zeros((BLK, BLK), F32)

    for copy in (get_row, get_off, get_diag, get_tiles):
        copy.wait()

    def reach(t, carry):
        r = trow[t]
        c = r + toff[t]

        @pl.when(c >= rowb)
        def _():
            tile = tiles[t]
            acc[r] += mm(jnp.concatenate([tile, tile], 1), pieces[c])

        return carry

    lax.fori_loop(0, count, reach, 0)

    count_ahead = from_ahead[2 * head : 2 * head + 1, :]
    for b in range(HB):
        at = slice(b * BLK, (b + 1) * BLK)
        row = rows_of(b).astype(F32)
        value = from_ahead[head + b * BLK : head + (b + 1) * BLK, :]
        value = value + jnp.where(row < count_ahead, behind[at, :], 0.0)
        high, low = split(value)
        pieces[rowb + b, :BLK, :] = high
        pieces[rowb + b, BLK:, :] = low

    def settle(b, extra):
        at = pl.ds(pl.multiple_of(b * BLK, BLK), BLK)
        value = part[at, :]
        if extra is not None:
            value = value + jnp.where(rows_of(b) < live, extra, 0.0)
        image[at, :] = value
        high, low = split(value)
        pieces[b, :BLK, :] = high
        pieces[b, BLK:, :] = low
        wide_h[at, BLK:] = high
        wide_l[at, BLK:] = low
        high, low = split(field[at, :])
        wide_h[at, :BLK] = high
        wide_l[at, :BLK] = low
        acc[b] = (0.5 * (column(diag[pl.ds(b, 1), :]) - SHIFT)) * value

    for b in range(HB):
        settle(b, from_behind[b * BLK : (b + 1) * BLK, :])
    for b in range(edge, rowb):
        settle(b, acc[b])

    def middle(b, carry):
        settle(b, None)
        return carry

    lax.fori_loop(HB, edge, middle, 0)

    def one(t):
        r = trow[t]
        tile = tiles[t]
        acc[r] += mm(jnp.concatenate([tile, tile], 1), pieces[r + toff[t]])

    tile_loop(count, 4, one)

    def widen(b, carry):
        at = pl.ds(pl.multiple_of(b * BLK, BLK), BLK)
        high, low = split(acc[b])
        u_h[at, :] = high
        u_l[at, :] = low
        return carry

    lax.fori_loop(0, rowb, widen, 0)

    first = ((0,), (0,))
    straight = mm(wide_h[...], wide_h[...], first)
    cross = mm(wide_h[...], wide_l[...], first)
    n0 = straight[:BLK, :BLK] + cross[:BLK, :BLK] + jnp.transpose(cross[:BLK, :BLK])
    n1 = straight[:BLK, BLK:] + cross[:BLK, BLK:] + jnp.transpose(cross[BLK:, :BLK])
    n2 = straight[BLK:, BLK:] + cross[BLK:, BLK:] + jnp.transpose(cross[BLK:, BLK:])
    half = mm(wide_h[:, BLK:], u_h[...], first)
    half = half + mm(wide_h[:, BLK:], u_l[...], first) + mm(wide_l[:, BLK:], u_h[...], first)
    n3 = half + jnp.transpose(half)
    n1 = 0.5 * (n1 + jnp.transpose(n1))
    low_packed, low_line = pack(n0, n1)
    high_packed, high_line = pack(n2, n3)

    def place(low_ref, high_ref):
        low_ref[:BLK, :] = low_packed
        low_ref[BLK:, :] = jnp.broadcast_to(low_line, (8, BLK))
        high_ref[:BLK, :] = high_packed
        high_ref[BLK:, :] = jnp.broadcast_to(high_line, (8, BLK))

    @pl.when(core[0] == 0)
    def _():
        place(keep, give)

    @pl.when(core[0] != 0)
    def _():
        place(give, keep)


def pivot_block(entry, n):
    for p in range(n):
        scale = pl.reciprocal(entry[p, p])
        old = {i: entry[min(i, p), max(i, p)] for i in range(n) if i != p}
        new = {i: value * scale for i, value in old.items()}
        for i in range(n):
            for j in range(i, n):
                if i == p and j == p:
                    entry[i, j] = -scale
                elif i == p or j == p:
                    entry[i, j] = new[i + j - p]
                else:
                    entry[i, j] = entry[i, j] - new[i] * old[j]
    return entry


def invert(matrix):
    n = matrix.shape[0]
    step = 8
    lane = lax.broadcasted_iota(jnp.int32, (step, n), 1)
    sub = lax.broadcasted_iota(jnp.int32, (step, n), 0)
    masks = [sub == i for i in range(step)]
    panel = matrix[:step, :]
    for k in range(n // step):
        base = k * step
        inside = (lane >= base) & (lane < base + step)
        columns = [
            jnp.broadcast_to(panel[:, base + j : base + j + 1], (step, n)) for j in range(step)
        ]
        entry = {
            (i, j): jnp.broadcast_to(columns[j][i : i + 1, :], (step, n))
            for i in range(step) for j in range(i, step)
        }
        entry = pivot_block(entry, step)
        rows = None
        unit = None
        for j in range(step):
            weight = entry[0, j]
            for i in range(1, step):
                weight = jnp.where(masks[i], entry[min(i, j), max(i, j)], weight)
            term = weight * panel[j : j + 1, :]
            rows = term if rows is None else rows + term
            spot = jnp.where(lane == base + j, weight, 0.0)
            unit = spot if unit is None else unit + spot
        rows = jnp.where(inside, unit, -rows)
        outer = jnp.where(inside, 0.0, panel)
        cleared = jnp.where(inside[:1, :], 0.0, matrix)
        if k + 1 < n // step:
            ahead = matrix[base + step : base + 2 * step, :]
            panel = cleared[base + step : base + 2 * step, :]
            for j in range(step):
                factor = jnp.broadcast_to(ahead[:, base + j : base + j + 1], (step, n))
                panel = panel - factor * rows[j : j + 1, :]
        matrix = cleared - mmh(outer, rows, ((0,), (0,)))
        pieces = []
        if base:
            pieces.append(matrix[:base, :])
        pieces.append(rows)
        if base + step < n:
            pieces.append(panel)
        if base + 2 * step < n:
            pieces.append(matrix[base + 2 * step :, :])
        matrix = jnp.concatenate(pieces, 0)
    return -matrix


def solve_kernel(core, mine, other, out):
    first = core[0] == 0
    low = jnp.where(first, mine[...], other[...])
    high = jnp.where(first, other[...], mine[...])
    n0, n1 = unpack(low[:BLK, :], low[BLK : BLK + 1, :])
    n2, n3 = unpack(high[:BLK, :], high[BLK : BLK + 1, :])
    m1 = n1 + SHIFT * n0
    m2 = n2 + SHIFT * n1
    m3 = n3 + SHIFT * n2
    inverse = invert(m1)
    both = mmh(inverse, jnp.concatenate([m2, n0], 1))
    across = mmh(m2, both)
    schur = m3 - across[:, :BLK]
    y1 = mmh(invert(schur), n1 - across[:, BLK:])
    y0 = both[:, BLK:] - mmh(both[:, :BLK], y1)
    out[:BLK, :] = y0
    out[BLK:, :] = y1


def third_kernel(irow, iblk, core, field, image, coef, inc, sol, keep, give, pieces):
    rowb = field.shape[0] // BLK
    y0h, y0l = split(coef[:BLK, :])
    y1h, y1l = split(coef[BLK:, :])
    stack_h = jnp.concatenate([y0h, y1h], 0)
    stack_l = jnp.concatenate([y0l, y1l], 0)
    keep[...] = jnp.zeros(keep.shape, F32)
    give[...] = jnp.zeros(give.shape, F32)

    def combine(b, carry):
        at = pl.ds(pl.multiple_of(b * BLK, BLK), BLK)
        fh, fl = split(field[at, :])
        ih, il = split(image[at, :])
        left_h = jnp.concatenate([fh, ih], 1)
        left_l = jnp.concatenate([fl, il], 1)
        value = mm(left_h, stack_h) + (mm(left_h, stack_l) + mm(left_l, stack_h))
        sol[at, :] = value
        high, low = split(value)
        pieces[b, :BLK, :] = high
        pieces[b, BLK:, :] = low
        return carry

    lax.fori_loop(0, rowb, combine, 0)

    def add(u, carry):
        flipped = jnp.transpose(inc[u])
        product = mm(jnp.concatenate([flipped, flipped], 1), pieces[irow[u]])
        block = iblk[u]
        owner = block // SRCB_DEV
        at = owner // 2 * SRCB_DEV + block % SRCB_DEV
        mine = owner % 2 == core[0]

        @pl.when(mine)
        def _():
            keep[at] += product

        @pl.when(jnp.logical_not(mine))
        def _():
            give[at] += product

        return carry

    lax.fori_loop(0, inc.shape[0], add, 0)


def call(kernel, n_scalar, n_far, n_vector, outs, scratch=(), mib=16):
    vmem = pl.BlockSpec(memory_space=pltpu.VMEM)
    smem = pl.BlockSpec(memory_space=pltpu.SMEM)
    far = pl.BlockSpec(memory_space=pltpu.HBM)
    return pl.pallas_call(
        kernel,
        in_specs=[smem] * n_scalar + [far] * n_far + [vmem] * n_vector,
        out_specs=[vmem] * len(outs),
        out_shape=[jax.ShapeDtypeStruct(shape, F32) for shape in outs],
        scratch_shapes=list(scratch),
        compiler_params=pltpu.CompilerParams(vmem_limit_bytes=mib * 1024 * 1024),
    )


def body(
    sides, rhs, diagonal, tile_values, tile_rows, tile_offsets, tile_count, node_count,
    inc_values, inc_rows, inc_blocks,
):
    nx, ny = sides
    nodes, width = rhs.shape
    rowb = nodes // BLK
    head = HB * BLK
    count = 2 * nx * ny
    lead_half = nx * ny * SRCB_DEV
    core = (lax.axis_index("mesh") % 2).astype(jnp.int32)[None]
    diag = diagonal.reshape(rowb, BLK)

    def place(x, y, c):
        return (x % nx * ny + y % ny) * 2 + c

    def moved(value, dx, dy):
        return lax.ppermute(value, "mesh", [
            (place(x, y, c), place(x + dx, y + dy, c))
            for x in range(nx) for y in range(ny) for c in range(2)
        ])

    def swap(value):
        return lax.ppermute(value, "mesh", [(i, i ^ 1) for i in range(count)])

    stay = functools.partial(pltpu.with_memory_space_constraint, memory_space=pltpu.HBM)
    slots = tile_values.shape[0]
    index = pltpu.SMEM((slots,), jnp.int32)
    lines = pltpu.VMEM((rowb, BLK), F32)
    tiles = pltpu.VMEM(tile_values.shape, BF16)
    acc = pltpu.VMEM((rowb + HB, BLK, BLK), F32)
    pieces = pltpu.VMEM((rowb + HB, 2 * BLK, BLK), BF16)
    field, part, ahead, behind = call(
        first_kernel, 2, 5, 0,
        [(nodes, width), (nodes, width), (2 * head + 8, width), (head, width)],
        [
            acc, pieces, index, index, pltpu.VMEM((nodes, width), F32), lines, tiles,
            pltpu.SemaphoreType.DMA((5,)),
        ],
    )(tile_count, node_count, *map(stay, (tile_rows, tile_offsets, rhs, diag, tile_values)))
    from_ahead = lax.ppermute(ahead, "mesh", [(i + 1, i) for i in range(count - 1)])
    from_behind = lax.ppermute(behind, "mesh", [(i, i + 1) for i in range(count - 1)])
    image, keep, give = call(
        second_kernel, 3, 4, 5,
        [(nodes, width), (BLK + 8, BLK), (BLK + 8, BLK)],
        [
            acc, pieces, pltpu.VMEM((nodes, 2 * BLK), BF16), pltpu.VMEM((nodes, 2 * BLK), BF16),
            pltpu.VMEM((nodes, BLK), BF16), pltpu.VMEM((nodes, BLK), BF16),
            index, index, lines, tiles, pltpu.SemaphoreType.DMA((4,)),
        ],
    )(tile_count, node_count, core, *map(stay, (tile_rows, tile_offsets, diag, tile_values)),
      field, part, behind, from_behind, from_ahead)
    total = keep + swap(give)
    total = total + functools.reduce(jnp.add, [moved(total, d, 0) for d in range(1, nx)])
    total = total + functools.reduce(jnp.add, [moved(total, 0, d) for d in range(1, ny)])
    (coef,) = call(solve_kernel, 1, 0, 2, [(2 * BLK, BLK)])(core, total, swap(total))
    solution, keep, give = call(
        third_kernel, 3, 0, 4,
        [(nodes, width), (lead_half, BLK, BLK), (lead_half, BLK, BLK)],
        [pltpu.VMEM((rowb, 2 * BLK, BLK), BF16)],
    )(inc_rows, inc_blocks, core, field, image, coef, inc_values)
    half = (keep + swap(give)).reshape(nx * ny, SRCB_DEV * BLK, width)
    groups = [[2 * i + c for i in range(nx * ny)] for c in range(2)]
    got = lax.all_to_all(
        half, "mesh", split_axis=0, concat_axis=0, tiled=True, axis_index_groups=groups
    )
    lead = lax.all_to_all(got.sum(0), "elec", split_axis=0, concat_axis=1, tiled=True)
    return solution, lead


def solution(mesh):
    placed = (
        P("mesh", "elec"),
        P("mesh"),
        P("mesh", None, None),
        P("mesh"),
        P("mesh"),
        P("mesh"),
        P("mesh"),
        P("mesh", None, None),
        P("mesh"),
        P("mesh"),
    )
    return jax.shard_map(
        functools.partial(body, (4, 4)),
        mesh=mesh,
        in_specs=placed,
        out_specs=(P("mesh", "elec"), P(("mesh", "elec"), None)),
        check_vma=False,
    )
```

```python
import functools

import jax
import jax.numpy as jnp
from jax import lax
from jax.experimental import pallas as pl
from jax.experimental.pallas import tpu as pltpu
from jax.sharding import PartitionSpec as P


HB = 2
SRCB_DEV = 2
BLK = 128
SHIFT = 2.0
F32 = jnp.float32
BF16 = jnp.bfloat16
HIGHEST = lax.Precision.HIGHEST
GROUP = 4


def mm(left, right, dims=((1,), (0,))):
    return lax.dot_general(left, right, (dims, ((), ())), preferred_element_type=F32)


def mmh(left, right, dims=((1,), (0,))):
    return lax.dot_general(
        left, right, (dims, ((), ())), preferred_element_type=F32, precision=HIGHEST
    )


def split(value):
    high = value.astype(BF16)
    return high, (value - high.astype(F32)).astype(BF16)


def rows_of(block):
    return block * BLK + lax.broadcasted_iota(jnp.int32, (BLK, BLK), 0)


def column(line):
    return jnp.transpose(jnp.broadcast_to(line, (BLK, BLK)))


def grouped(count, one):
    def group(g, carry):
        for add in [one(g * GROUP + k, g * GROUP + k < count) for k in range(GROUP)]:
            for target, index, value in add:
                target[index] += value
        return carry

    lax.fori_loop(0, (count + GROUP - 1) // GROUP, group, 0)


def chosen_loop(count, trow, toff, chosen, wanted, one):
    def scan(t, n):
        chosen[n] = t
        r = trow[t]
        return n + wanted(r, r + toff[t]).astype(jnp.int32)

    n = lax.fori_loop(0, count, scan, 0)
    grouped(n, lambda k, live: one(chosen[jnp.minimum(k, n - 1)], live))


def block_loop(first, last, one):
    steps = (last - first) // GROUP

    def group(g, carry):
        for k in range(GROUP):
            one(first + g * GROUP + k)
        return carry

    lax.fori_loop(0, steps, group, 0)
    for b in range(first + steps * GROUP, last):
        one(b)


def block_at(b):
    return pl.ds(pl.multiple_of(b * BLK, BLK), BLK)


def halves(pieces, b, value):
    high, low = split(value)
    pieces[b, :BLK, :] = high
    pieces[b, BLK:, :] = low
    return high, low


def forward(tile, piece):
    return mm(jnp.concatenate([tile, tile], 1), piece)


def backward(tile, piece):
    flipped = jnp.transpose(tile)
    return mm(jnp.concatenate([flipped, flipped], 1), piece)


def fetch(pairs, sems):
    copies = [
        pltpu.make_async_copy(source, target, sems.at[i])
        for i, (source, target) in enumerate(pairs)
    ]
    for copy in copies:
        copy.start()
    return copies


def edge_kernel(
    tcount, ncount, trow_far, toff_far, rhs_far, diag_far, tiles_far,
    ahead, behind, acc, pieces, chosen, trow, toff, rhs, diag, tiles, sems,
):
    head = HB * BLK
    nodes = rhs_far.shape[0]
    rowb = nodes // BLK
    low, high = slice(0, 2 * head), slice(nodes - head, nodes)
    get_low, get_high, get_diag, get_row, get_off, get_tiles = fetch(
        [
            (rhs_far.at[low], rhs.at[low]), (rhs_far.at[high], rhs.at[high]), (diag_far, diag),
            (trow_far, trow), (toff_far, toff), (tiles_far, tiles),
        ],
        sems,
    )
    live = ncount[0]
    spare = 2 * HB
    for copy in (get_low, get_high, get_diag):
        copy.wait()
    for b in [*range(2 * HB), *range(rowb - HB, rowb)]:
        value = jnp.where(rows_of(b) < live, rhs[b * BLK : (b + 1) * BLK, :], 0.0)
        halves(pieces, b, value)
        if b < HB:
            ahead[b * BLK : (b + 1) * BLK, :] = value
            acc[b] = (column(diag[b : b + 1, :]) - SHIFT) * value
    for b in range(HB, 2 * HB):
        acc[b] = jnp.zeros((BLK, BLK), F32)
    for copy in (get_row, get_off, get_tiles):
        copy.wait()

    def one(t, on):
        r = trow[t]
        c = r + toff[t]
        tile = tiles[t]
        inner = jnp.minimum(c, rowb - 1)
        to_row = jnp.where(on & (r < HB), r, spare)
        to_col = jnp.where(c >= rowb, c - rowb + HB, jnp.where(c < HB, c, spare))
        return (
            (acc, to_row, forward(tile, pieces[inner])),
            (acc, jnp.where(on, to_col, spare), backward(tile, pieces[r])),
        )

    chosen_loop(tcount[0], trow, toff, chosen, lambda r, c: (r < HB) | (c >= rowb), one)
    for b in range(HB):
        at = slice(head + b * BLK, head + (b + 1) * BLK)
        ahead[at, :] = jnp.where(rows_of(b) < live, acc[b], 0.0)
        behind[b * BLK : (b + 1) * BLK, :] = acc[HB + b]
    ahead[2 * head :, :] = jnp.full((8, BLK), live.astype(F32))


def first_kernel(
    tcount, ncount, trow_far, toff_far, rhs_far, diag_far, tiles_far,
    field, part, acc, pieces, trow, toff, rhs, diag, tiles, sems,
):
    get_rhs, get_diag, get_row, get_off, get_tiles = fetch(
        [(rhs_far, rhs), (diag_far, diag), (trow_far, trow), (toff_far, toff), (tiles_far, tiles)],
        sems,
    )
    get_rhs.wait()
    get_diag.wait()
    rowb = rhs.shape[0] // BLK
    live = ncount[0]
    spare = rowb

    def prepare(b):
        value = jnp.where(rows_of(b) < live, rhs[block_at(b), :], 0.0)
        field[block_at(b), :] = value
        halves(pieces, b, value)
        acc[b] = (column(diag[pl.ds(b, 1), :]) - SHIFT) * value

    block_loop(0, rowb, prepare)
    for copy in (get_row, get_off, get_tiles):
        copy.wait()

    def one(t, on):
        r = trow[t]
        c = r + toff[t]
        tile = tiles[t]
        inside = on & (c < rowb)
        return (
            (acc, jnp.where(inside, r, spare), forward(tile, pieces[jnp.minimum(c, rowb - 1)])),
            (acc, jnp.where(inside, c, spare), backward(tile, pieces[r])),
        )

    grouped(tcount[0], one)

    def finish(b):
        part[block_at(b), :] = jnp.where(rows_of(b) < live, acc[b], 0.0)

    block_loop(0, rowb, finish)


def pack(first, second):
    i = lax.broadcasted_iota(jnp.int32, (BLK, BLK), 0)
    j = lax.broadcasted_iota(jnp.int32, (BLK, BLK), 1)
    line = jnp.sum(jnp.where(i == j, second, 0.0), 0, keepdims=True)
    return jnp.where(i <= j, first, second), line


def unpack(packed, line):
    i = lax.broadcasted_iota(jnp.int32, (BLK, BLK), 0)
    j = lax.broadcasted_iota(jnp.int32, (BLK, BLK), 1)
    flipped = jnp.transpose(packed)
    first = jnp.where(i <= j, packed, flipped)
    second = jnp.where(i > j, packed, flipped)
    return first, jnp.where(i == j, jnp.broadcast_to(line, (BLK, BLK)), second)


def second_kernel(
    tcount, ncount, core,
    trow_far, toff_far, diag_far, tiles_far, field, part, behind, from_behind, from_ahead,
    wide_h, wide_l, keep, give, acc, pieces, u_h, u_l, chosen, trow, toff, diag, tiles, sems,
):
    get_row, get_off, get_diag, get_tiles = fetch(
        [(trow_far, trow), (toff_far, toff), (diag_far, diag), (tiles_far, tiles)], sems
    )
    rowb = field.shape[0] // BLK
    live = ncount[0]
    count = tcount[0]
    head = HB * BLK
    edge = rowb - HB
    spare = rowb

    for b in range(HB):
        halves(pieces, rowb + b, from_ahead[b * BLK : (b + 1) * BLK, :])
        acc[edge + b] = jnp.zeros((BLK, BLK), F32)

    for copy in (get_row, get_off, get_diag, get_tiles):
        copy.wait()

    def reach(t, on):
        r = trow[t]
        value = forward(tiles[t], pieces[r + toff[t]])
        return ((acc, jnp.where(on, r, spare), value),)

    chosen_loop(count, trow, toff, chosen, lambda r, c: c >= rowb, reach)

    count_ahead = from_ahead[2 * head : 2 * head + 1, :]
    for b in range(HB):
        at = slice(b * BLK, (b + 1) * BLK)
        row = rows_of(b).astype(F32)
        value = from_ahead[head + b * BLK : head + (b + 1) * BLK, :]
        halves(pieces, rowb + b, value + jnp.where(row < count_ahead, behind[at, :], 0.0))

    def settle(b, extra=None):
        at = block_at(b)
        value = part[at, :]
        if extra is not None:
            value = value + jnp.where(rows_of(b) < live, extra, 0.0)
        high, low = halves(pieces, b, value)
        wide_h[at, BLK:] = high
        wide_l[at, BLK:] = low
        high, low = split(field[at, :])
        wide_h[at, :BLK] = high
        wide_l[at, :BLK] = low
        acc[b] = (0.5 * (column(diag[pl.ds(b, 1), :]) - SHIFT)) * value

    for b in range(HB):
        settle(b, from_behind[b * BLK : (b + 1) * BLK, :])
    for b in range(edge, rowb):
        settle(b, acc[b])
    block_loop(HB, edge, settle)

    def one(t, on):
        r = trow[t]
        value = forward(tiles[t], pieces[r + toff[t]])
        return ((acc, jnp.where(on, r, spare), value),)

    grouped(count, one)

    def widen(b):
        high, low = split(acc[b])
        u_h[block_at(b), :] = high
        u_l[block_at(b), :] = low

    block_loop(0, rowb, widen)

    first = ((0,), (0,))
    straight = mm(wide_h[...], wide_h[...], first)
    cross = mm(wide_h[...], wide_l[...], first)
    n0 = straight[:BLK, :BLK] + cross[:BLK, :BLK] + jnp.transpose(cross[:BLK, :BLK])
    n1 = straight[:BLK, BLK:] + cross[:BLK, BLK:] + jnp.transpose(cross[BLK:, :BLK])
    n2 = straight[BLK:, BLK:] + cross[BLK:, BLK:] + jnp.transpose(cross[BLK:, BLK:])
    half = mm(wide_h[:, BLK:], u_h[...], first)
    half = half + mm(wide_h[:, BLK:], u_l[...], first) + mm(wide_l[:, BLK:], u_h[...], first)
    n3 = half + jnp.transpose(half)
    n1 = 0.5 * (n1 + jnp.transpose(n1))
    low_packed, low_line = pack(n0, n1)
    high_packed, high_line = pack(n2, n3)

    def place(low_ref, high_ref):
        low_ref[:BLK, :] = low_packed
        low_ref[BLK:, :] = jnp.broadcast_to(low_line, (8, BLK))
        high_ref[:BLK, :] = high_packed
        high_ref[BLK:, :] = jnp.broadcast_to(high_line, (8, BLK))

    @pl.when(core[0] == 0)
    def _():
        place(keep, give)

    @pl.when(core[0] != 0)
    def _():
        place(give, keep)


def pivot_block(entry, n):
    for p in range(n):
        scale = pl.reciprocal(entry[p, p])
        old = {i: entry[min(i, p), max(i, p)] for i in range(n) if i != p}
        new = {i: value * scale for i, value in old.items()}
        for i in range(n):
            for j in range(i, n):
                if i == p and j == p:
                    entry[i, j] = -scale
                elif i == p or j == p:
                    entry[i, j] = new[i + j - p]
                else:
                    entry[i, j] = entry[i, j] - new[i] * old[j]
    return entry


def thirds(value):
    high = value.astype(BF16).astype(F32)
    rest = value - high
    middle = rest.astype(BF16).astype(F32)
    return high, middle, rest - middle


def stacked(left, right):
    lh, lm, ll = thirds(left)
    rh, rm, rl = thirds(right)
    lefts = jnp.concatenate([lh, lh, lh, lm, lm, ll], 0).astype(BF16)
    rights = jnp.concatenate([rh, rm, rl, rh, rm, rh], 0).astype(BF16)
    return mm(lefts, rights, ((0,), (0,)))


def invert(matrix):
    n = matrix.shape[0]
    step = 8
    lane = lax.broadcasted_iota(jnp.int32, (step, n), 1)
    sub = lax.broadcasted_iota(jnp.int32, (step, n), 0)
    masks = [sub == i for i in range(step)]
    panel = matrix[:step, :]
    for k in range(n // step):
        base = k * step
        inside = (lane >= base) & (lane < base + step)
        columns = [
            jnp.broadcast_to(panel[:, base + j : base + j + 1], (step, n)) for j in range(step)
        ]
        entry = {
            (i, j): jnp.broadcast_to(columns[j][i : i + 1, :], (step, n))
            for i in range(step) for j in range(i, step)
        }
        entry = pivot_block(entry, step)
        rows = None
        unit = None
        for j in range(step):
            weight = entry[0, j]
            for i in range(1, step):
                weight = jnp.where(masks[i], entry[min(i, j), max(i, j)], weight)
            term = weight * panel[j : j + 1, :]
            rows = term if rows is None else rows + term
            spot = jnp.where(lane == base + j, weight, 0.0)
            unit = spot if unit is None else unit + spot
        rows = jnp.where(inside, unit, -rows)
        outer = jnp.where(inside, 0.0, panel)
        cleared = jnp.where(inside[:1, :], 0.0, matrix)
        if k + 1 < n // step:
            ahead = matrix[base + step : base + 2 * step, :]
            panel = cleared[base + step : base + 2 * step, :]
            for j in range(step):
                factor = jnp.broadcast_to(ahead[:, base + j : base + j + 1], (step, n))
                panel = panel - factor * rows[j : j + 1, :]
        matrix = cleared - stacked(outer, rows)
        pieces = []
        if base:
            pieces.append(matrix[:base, :])
        pieces.append(rows)
        if base + step < n:
            pieces.append(panel)
        if base + 2 * step < n:
            pieces.append(matrix[base + 2 * step :, :])
        matrix = jnp.concatenate(pieces, 0)
    return -matrix


def solve_kernel(core, mine, other, out):
    first = core[0] == 0
    low = jnp.where(first, mine[...], other[...])
    high = jnp.where(first, other[...], mine[...])
    n0, n1 = unpack(low[:BLK, :], low[BLK : BLK + 1, :])
    n2, n3 = unpack(high[:BLK, :], high[BLK : BLK + 1, :])
    m1 = n1 + SHIFT * n0
    m2 = n2 + SHIFT * n1
    m3 = n3 + SHIFT * n2
    inverse = invert(m1)
    both = mmh(inverse, jnp.concatenate([m2, n0], 1))
    across = mmh(m2, both)
    schur = m3 - across[:, :BLK]
    y1 = mmh(invert(schur), n1 - across[:, BLK:])
    y0 = both[:, BLK:] - mmh(both[:, :BLK], y1)
    out[:BLK, :] = y0
    out[BLK:, :] = y1


def gather_kernel(irow, wide_h, wide_l, inc, out_h, out_l):
    for u in range(inc.shape[0]):
        at = block_at(irow[u])
        value = backward(inc[u], jnp.concatenate([wide_h[at, :], wide_l[at, :]], 0))
        high, low = split(value)
        out_h[u * BLK : (u + 1) * BLK, :] = high
        out_l[u * BLK : (u + 1) * BLK, :] = low


def combine(left_h, left_l, coef):
    high, low = split(coef)
    return mm(left_h, high) + (mm(left_h, low) + mm(left_l, high))


def scatter_kernel(iblk, core, left_h, left_l, coef, keep, give):
    keep[...] = jnp.zeros(keep.shape, F32)
    give[...] = jnp.zeros(give.shape, F32)
    weights = coef[...]
    for g in range(left_h.shape[0] // (GROUP * BLK)):
        at = slice(g * GROUP * BLK, (g + 1) * GROUP * BLK)
        product = combine(left_h[at, :], left_l[at, :], weights)
        for k in range(GROUP):
            value = product[k * BLK : (k + 1) * BLK, :]
            block = iblk[g * GROUP + k]
            owner = block // SRCB_DEV
            to = owner // 2 * SRCB_DEV + block % SRCB_DEV
            mine = owner % 2 == core[0]

            @pl.when(mine)
            def _():
                keep[to] += value

            @pl.when(jnp.logical_not(mine))
            def _():
                give[to] += value


def third_kernel(left_h, left_l, coef, sol):
    weights = coef[...]
    step = GROUP * BLK
    for g in range(sol.shape[0] // step):
        at = slice(g * step, (g + 1) * step)
        sol[at, :] = combine(left_h[at, :], left_l[at, :], weights)


def call(kernel, n_scalar, n_far, n_vector, outs, scratch=(), mib=16):
    vmem = pl.BlockSpec(memory_space=pltpu.VMEM)
    smem = pl.BlockSpec(memory_space=pltpu.SMEM)
    far = pl.BlockSpec(memory_space=pltpu.HBM)
    return pl.pallas_call(
        kernel,
        in_specs=[smem] * n_scalar + [far] * n_far + [vmem] * n_vector,
        out_specs=[vmem] * len(outs),
        out_shape=[jax.ShapeDtypeStruct(shape, (list(kind) or [F32])[0]) for shape, *kind in outs],
        scratch_shapes=list(scratch),
        compiler_params=pltpu.CompilerParams(vmem_limit_bytes=mib * 1024 * 1024),
    )


def body(
    sides, rhs, diagonal, tile_values, tile_rows, tile_offsets, tile_count, node_count,
    inc_values, inc_rows, inc_blocks,
):
    nx, ny = sides
    nodes, width = rhs.shape
    rowb = nodes // BLK
    head = HB * BLK
    count = 2 * nx * ny
    lead_half = nx * ny * SRCB_DEV
    core = (lax.axis_index("mesh") % 2).astype(jnp.int32)[None]
    diag = diagonal.reshape(rowb, BLK)

    def place(x, y, c):
        return (x % nx * ny + y % ny) * 2 + c

    def moved(value, dx, dy):
        return lax.ppermute(value, "mesh", [
            (place(x, y, c), place(x + dx, y + dy, c))
            for x in range(nx) for y in range(ny) for c in range(2)
        ])

    def swap(value):
        return lax.ppermute(value, "mesh", [(i, i ^ 1) for i in range(count)])

    stay = functools.partial(pltpu.with_memory_space_constraint, memory_space=pltpu.HBM)
    slots = tile_values.shape[0]
    index = pltpu.SMEM((slots,), jnp.int32)
    lines = pltpu.VMEM((rowb, BLK), F32)
    tiles = pltpu.VMEM(tile_values.shape, BF16)
    acc = pltpu.VMEM((rowb + 1, BLK, BLK), F32)
    pieces = pltpu.VMEM((rowb + HB, 2 * BLK, BLK), BF16)
    chosen = index
    tile_args = (tile_count, node_count, *map(stay, (tile_rows, tile_offsets, rhs, diag, tile_values)))
    held = [index, index, pltpu.VMEM((nodes, width), F32), lines, tiles]
    ahead, behind = call(
        edge_kernel, 2, 5, 0,
        [((2 * head + 8, width),), ((head, width),)],
        [
            pltpu.VMEM((2 * HB + 1, BLK, BLK), F32), pieces, chosen, *held,
            pltpu.SemaphoreType.DMA((6,)),
        ],
    )(*tile_args)
    from_ahead = lax.ppermute(ahead, "mesh", [(i + 1, i) for i in range(count - 1)])
    from_behind = lax.ppermute(behind, "mesh", [(i, i + 1) for i in range(count - 1)])
    field, part = call(
        first_kernel, 2, 5, 0,
        [((nodes, width),), ((nodes, width),)],
        [acc, pieces, *held, pltpu.SemaphoreType.DMA((5,))],
    )(*tile_args)
    wide_h, wide_l, keep, give = call(
        second_kernel, 3, 4, 5,
        [((nodes, 2 * BLK), BF16), ((nodes, 2 * BLK), BF16), ((BLK + 8, BLK),), ((BLK + 8, BLK),)],
        [
            acc, pieces, pltpu.VMEM((nodes, BLK), BF16), pltpu.VMEM((nodes, BLK), BF16),
            chosen, index, index, lines, tiles, pltpu.SemaphoreType.DMA((4,)),
        ],
    )(tile_count, node_count, core, *map(stay, (tile_rows, tile_offsets, diag, tile_values)),
      field, part, behind, from_behind, from_ahead)
    total = keep + swap(give)
    total = total + functools.reduce(jnp.add, [moved(total, d, 0) for d in range(1, nx)])
    total = total + functools.reduce(jnp.add, [moved(total, 0, d) for d in range(1, ny)])
    other = swap(total)
    rows = inc_values.shape[0] * BLK
    gather_h, gather_l = call(
        gather_kernel, 1, 0, 3, [((rows, 2 * BLK), BF16), ((rows, 2 * BLK), BF16)]
    )(inc_rows, wide_h, wide_l, inc_values)
    (coef,) = call(solve_kernel, 1, 0, 2, [((2 * BLK, BLK),)])(core, total, other)
    keep, give = call(scatter_kernel, 2, 0, 3, [((lead_half, BLK, BLK),)] * 2)(
        inc_blocks, core, gather_h, gather_l, coef
    )
    other = swap(give)
    (solution,) = call(third_kernel, 0, 0, 3, [((nodes, width),)])(wide_h, wide_l, coef)
    half = (keep + other).reshape(nx * ny, SRCB_DEV * BLK, width)
    groups = [[2 * i + c for i in range(nx * ny)] for c in range(2)]
    got = lax.all_to_all(
        half, "mesh", split_axis=0, concat_axis=0, tiled=True, axis_index_groups=groups
    )
    lead = lax.all_to_all(got.sum(0), "elec", split_axis=0, concat_axis=1, tiled=True)
    return solution, lead


def solution(mesh):
    placed = (
        P("mesh", "elec"),
        P("mesh"),
        P("mesh", None, None),
        P("mesh"),
        P("mesh"),
        P("mesh"),
        P("mesh"),
        P("mesh", None, None),
        P("mesh"),
        P("mesh"),
    )

    def whole(*args):
        return body((4, 4), *args)

    return jax.shard_map(
        whole,
        mesh=mesh,
        in_specs=placed,
        out_specs=(P("mesh", "elec"), P(("mesh", "elec"), None)),
        check_vma=False,
    )
```

```python
import functools

import jax
import jax.numpy as jnp
from jax import lax
from jax.experimental import pallas as pl
from jax.experimental.pallas import tpu as pltpu
from jax.sharding import PartitionSpec as P


HB = 2
SRCB_DEV = 2
BLK = 128
SHIFT = 2.0
F32 = jnp.float32
BF16 = jnp.bfloat16
HIGHEST = lax.Precision.HIGHEST
GROUP = 4


def mm(left, right, dims=((1,), (0,))):
    return lax.dot_general(left, right, (dims, ((), ())), preferred_element_type=F32)


def mmh(left, right, dims=((1,), (0,))):
    return lax.dot_general(
        left, right, (dims, ((), ())), preferred_element_type=F32, precision=HIGHEST
    )


def split(value):
    high = value.astype(BF16)
    return high, (value - high.astype(F32)).astype(BF16)


def rows_of(block):
    return block * BLK + lax.broadcasted_iota(jnp.int32, (BLK, BLK), 0)


def column(line):
    return jnp.transpose(jnp.broadcast_to(line, (BLK, BLK)))


def grouped(count, one):
    def group(g, carry):
        for add in [one(g * GROUP + k, g * GROUP + k < count) for k in range(GROUP)]:
            for target, index, value in add:
                target[index] += value
        return carry

    lax.fori_loop(0, (count + GROUP - 1) // GROUP, group, 0)


def chosen_loop(count, trow, toff, chosen, wanted, one):
    def scan(t, n):
        chosen[n] = t
        r = trow[t]
        return n + wanted(r, r + toff[t]).astype(jnp.int32)

    n = lax.fori_loop(0, count, scan, 0)
    grouped(n, lambda k, live: one(chosen[jnp.minimum(k, n - 1)], live))


def block_loop(first, last, one):
    steps = (last - first) // GROUP

    def group(g, carry):
        for k in range(GROUP):
            one(first + g * GROUP + k)
        return carry

    lax.fori_loop(0, steps, group, 0)
    for b in range(first + steps * GROUP, last):
        one(b)


def block_at(b):
    return pl.ds(pl.multiple_of(b * BLK, BLK), BLK)


def halves(pieces, b, value):
    high, low = split(value)
    pieces[b, :BLK, :] = high
    pieces[b, BLK:, :] = low
    return high, low


def forward(tile, piece):
    return mm(jnp.concatenate([tile, tile], 1), piece)


def backward(tile, piece):
    flipped = jnp.transpose(tile)
    return mm(jnp.concatenate([flipped, flipped], 1), piece)


def fetch(pairs, sems):
    copies = [
        pltpu.make_async_copy(source, target, sems.at[i])
        for i, (source, target) in enumerate(pairs)
    ]
    for copy in copies:
        copy.start()
    return copies


def edge_kernel(
    tcount, ncount, core, trow_far, toff_far, rhs_far, diag_far, tiles_far,
    behind, to_chip, to_next, ahead, acc, pieces, chosen, trow, toff, rhs, diag, tiles, sems,
):
    head = HB * BLK
    nodes = rhs_far.shape[0]
    rowb = nodes // BLK
    low, high = slice(0, 2 * head), slice(nodes - head, nodes)
    get_low, get_high, get_diag, get_row, get_off, get_tiles = fetch(
        [
            (rhs_far.at[low], rhs.at[low]), (rhs_far.at[high], rhs.at[high]), (diag_far, diag),
            (trow_far, trow), (toff_far, toff), (tiles_far, tiles),
        ],
        sems,
    )
    live = ncount[0]
    spare = 2 * HB
    for copy in (get_low, get_high, get_diag):
        copy.wait()
    for b in [*range(2 * HB), *range(rowb - HB, rowb)]:
        value = jnp.where(rows_of(b) < live, rhs[b * BLK : (b + 1) * BLK, :], 0.0)
        halves(pieces, b, value)
        if b < HB:
            ahead[b * BLK : (b + 1) * BLK, :] = value
            acc[b] = (column(diag[b : b + 1, :]) - SHIFT) * value
    for b in range(HB, 2 * HB):
        acc[b] = jnp.zeros((BLK, BLK), F32)
    for copy in (get_row, get_off, get_tiles):
        copy.wait()

    def one(t, on):
        r = trow[t]
        c = r + toff[t]
        tile = tiles[t]
        inner = jnp.minimum(c, rowb - 1)
        to_row = jnp.where(on & (r < HB), r, spare)
        to_col = jnp.where(c >= rowb, c - rowb + HB, jnp.where(c < HB, c, spare))
        return (
            (acc, to_row, forward(tile, pieces[inner])),
            (acc, jnp.where(on, to_col, spare), backward(tile, pieces[r])),
        )

    chosen_loop(tcount[0], trow, toff, chosen, lambda r, c: (r < HB) | (c >= rowb), one)
    for b in range(HB):
        at = slice(head + b * BLK, head + (b + 1) * BLK)
        ahead[at, :] = jnp.where(rows_of(b) < live, acc[b], 0.0)
        behind[b * BLK : (b + 1) * BLK, :] = acc[HB + b]
    ahead[2 * head :, :] = jnp.full((8, BLK), live.astype(F32))

    def place(lower, upper):
        lower[...] = ahead[...]
        upper[:head, :] = behind[...]
        upper[head:, :] = jnp.zeros((head + 8, BLK), F32)

    @pl.when(core[0] == 0)
    def _():
        place(to_next, to_chip)

    @pl.when(core[0] != 0)
    def _():
        place(to_chip, to_next)


def first_kernel(
    tcount, ncount, trow_far, toff_far, rhs_far, diag_far, tiles_far,
    field, part, acc, pieces, trow, toff, rhs, diag, tiles, sems,
):
    get_rhs, get_diag, get_row, get_off, get_tiles = fetch(
        [(rhs_far, rhs), (diag_far, diag), (trow_far, trow), (toff_far, toff), (tiles_far, tiles)],
        sems,
    )
    get_rhs.wait()
    get_diag.wait()
    rowb = rhs.shape[0] // BLK
    live = ncount[0]
    spare = rowb

    def prepare(b):
        value = jnp.where(rows_of(b) < live, rhs[block_at(b), :], 0.0)
        field[block_at(b), :] = value
        halves(pieces, b, value)
        acc[b] = (column(diag[pl.ds(b, 1), :]) - SHIFT) * value

    block_loop(0, rowb, prepare)
    for copy in (get_row, get_off, get_tiles):
        copy.wait()

    def one(t, on):
        r = trow[t]
        c = r + toff[t]
        tile = tiles[t]
        inside = on & (c < rowb)
        return (
            (acc, jnp.where(inside, r, spare), forward(tile, pieces[jnp.minimum(c, rowb - 1)])),
            (acc, jnp.where(inside, c, spare), backward(tile, pieces[r])),
        )

    grouped(tcount[0], one)

    def finish(b):
        part[block_at(b), :] = jnp.where(rows_of(b) < live, acc[b], 0.0)

    block_loop(0, rowb, finish)


def pack(first, second):
    i = lax.broadcasted_iota(jnp.int32, (BLK, BLK), 0)
    j = lax.broadcasted_iota(jnp.int32, (BLK, BLK), 1)
    line = jnp.sum(jnp.where(i == j, second, 0.0), 0, keepdims=True)
    return jnp.where(i <= j, first, second), line


def unpack(packed, line):
    i = lax.broadcasted_iota(jnp.int32, (BLK, BLK), 0)
    j = lax.broadcasted_iota(jnp.int32, (BLK, BLK), 1)
    flipped = jnp.transpose(packed)
    first = jnp.where(i <= j, packed, flipped)
    second = jnp.where(i > j, packed, flipped)
    return first, jnp.where(i == j, jnp.broadcast_to(line, (BLK, BLK)), second)


def second_kernel(
    tcount, ncount, core,
    trow_far, toff_far, diag_far, tiles_far, field, part, behind, from_chip, from_next,
    wide_h, wide_l, keep, give, acc, pieces, wide_u, chosen, trow, toff, diag, tiles, sems,
):
    get_row, get_off, get_diag, get_tiles = fetch(
        [(trow_far, trow), (toff_far, toff), (diag_far, diag), (tiles_far, tiles)], sems
    )
    rowb = field.shape[0] // BLK
    live = ncount[0]
    count = tcount[0]
    head = HB * BLK
    edge = rowb - HB
    spare = rowb
    even = core[0] == 0
    from_ahead = jnp.where(even, from_chip[...], from_next[...])
    from_behind = jnp.where(even, from_next[:head, :], from_chip[:head, :])

    for b in range(HB):
        halves(pieces, rowb + b, from_ahead[b * BLK : (b + 1) * BLK, :])
        acc[edge + b] = jnp.zeros((BLK, BLK), F32)

    for copy in (get_row, get_off, get_diag, get_tiles):
        copy.wait()

    def reach(t, on):
        r = trow[t]
        value = forward(tiles[t], pieces[r + toff[t]])
        return ((acc, jnp.where(on, r, spare), value),)

    chosen_loop(count, trow, toff, chosen, lambda r, c: c >= rowb, reach)

    count_ahead = from_ahead[2 * head : 2 * head + 1, :]
    for b in range(HB):
        at = slice(b * BLK, (b + 1) * BLK)
        row = rows_of(b).astype(F32)
        value = from_ahead[head + b * BLK : head + (b + 1) * BLK, :]
        halves(pieces, rowb + b, value + jnp.where(row < count_ahead, behind[at, :], 0.0))

    def settle(b, extra=None):
        at = block_at(b)
        value = part[at, :]
        if extra is not None:
            value = value + jnp.where(rows_of(b) < live, extra, 0.0)
        high, low = halves(pieces, b, value)
        wide_h[at, BLK:] = high
        wide_l[at, BLK:] = low
        high, low = split(field[at, :])
        wide_h[at, :BLK] = high
        wide_l[at, :BLK] = low
        acc[b] = (0.5 * (column(diag[pl.ds(b, 1), :]) - SHIFT)) * value

    for b in range(HB):
        settle(b, from_behind[b * BLK : (b + 1) * BLK, :])
    for b in range(edge, rowb):
        settle(b, acc[b])
    block_loop(HB, edge, settle)

    def one(t, on):
        r = trow[t]
        value = forward(tiles[t], pieces[r + toff[t]])
        return ((acc, jnp.where(on, r, spare), value),)

    grouped(count, one)

    def widen(b):
        high, low = split(acc[b])
        wide_u[block_at(b), :BLK] = high
        wide_u[block_at(b), BLK:] = low

    block_loop(0, rowb, widen)

    first = ((0,), (0,))
    straight = mm(wide_h[...], wide_h[...], first)
    cross = mm(wide_h[...], wide_l[...], first)
    n0 = straight[:BLK, :BLK] + cross[:BLK, :BLK] + jnp.transpose(cross[:BLK, :BLK])
    n1 = straight[:BLK, BLK:] + cross[:BLK, BLK:] + jnp.transpose(cross[BLK:, :BLK])
    n2 = straight[BLK:, BLK:] + cross[BLK:, BLK:] + jnp.transpose(cross[BLK:, BLK:])
    both = mm(wide_h[:, BLK:], wide_u[...], first)
    half = both[:, :BLK] + both[:, BLK:] + mm(wide_l[:, BLK:], wide_u[:, :BLK], first)
    n3 = half + jnp.transpose(half)
    n1 = 0.5 * (n1 + jnp.transpose(n1))
    low_packed, low_line = pack(n0, n1)
    high_packed, high_line = pack(n2, n3)

    def place(low_ref, high_ref):
        low_ref[:BLK, :] = low_packed
        low_ref[BLK:, :] = jnp.broadcast_to(low_line, (8, BLK))
        high_ref[:BLK, :] = high_packed
        high_ref[BLK:, :] = jnp.broadcast_to(high_line, (8, BLK))

    @pl.when(core[0] == 0)
    def _():
        place(keep, give)

    @pl.when(core[0] != 0)
    def _():
        place(give, keep)


def pivot_block(columns):
    n = len(columns)
    sub = lax.broadcasted_iota(jnp.int32, columns[0].shape, 0)
    for p in range(n):
        here = sub == p
        row = [jnp.broadcast_to(value[p : p + 1, :], value.shape) for value in columns]
        scale = pl.reciprocal(row[p])
        factor = jnp.where(here, -scale, columns[p] * scale)
        columns = [
            factor if j == p else jnp.where(here, 0.0, columns[j]) - factor * row[j]
            for j in range(n)
        ]
    return columns


def thirds(value):
    high = value.astype(BF16).astype(F32)
    rest = value - high
    middle = rest.astype(BF16).astype(F32)
    return high, middle, rest - middle


def stacked(left, right):
    lh, lm, ll = thirds(left)
    rh, rm, rl = thirds(right)
    lefts = jnp.concatenate([lh, lh, lh, lm, lm, ll], 0).astype(BF16)
    rights = jnp.concatenate([rh, rm, rl, rh, rm, rh], 0).astype(BF16)
    return mm(lefts, rights, ((0,), (0,)))


def invert(matrix):
    n = matrix.shape[0]
    step = 8
    lane = lax.broadcasted_iota(jnp.int32, (step, n), 1)
    panel = matrix[:step, :]
    for k in range(n // step):
        base = k * step
        inside = (lane >= base) & (lane < base + step)
        columns = [
            jnp.broadcast_to(panel[:, base + j : base + j + 1], (step, n)) for j in range(step)
        ]
        columns = pivot_block(columns)
        rows = None
        unit = columns[0]
        for j in range(step):
            term = columns[j] * panel[j : j + 1, :]
            rows = term if rows is None else rows + term
            unit = jnp.where(lane == base + j, columns[j], unit)
        rows = jnp.where(inside, unit, -rows)
        outer = jnp.where(inside, 0.0, panel)
        cleared = jnp.where(inside[:1, :], 0.0, matrix)
        if k + 1 < n // step:
            ahead = matrix[base + step : base + 2 * step, :]
            panel = cleared[base + step : base + 2 * step, :]
            for j in range(step):
                factor = jnp.broadcast_to(ahead[:, base + j : base + j + 1], (step, n))
                panel = panel - factor * rows[j : j + 1, :]
        matrix = cleared - stacked(outer, rows)
        pieces = []
        if base:
            pieces.append(matrix[:base, :])
        pieces.append(rows)
        if base + step < n:
            pieces.append(panel)
        if base + 2 * step < n:
            pieces.append(matrix[base + 2 * step :, :])
        matrix = jnp.concatenate(pieces, 0)
    return -matrix


def solve_kernel(core, mine, other, out):
    first = core[0] == 0
    low = jnp.where(first, mine[...], other[...])
    high = jnp.where(first, other[...], mine[...])
    n0, n1 = unpack(low[:BLK, :], low[BLK : BLK + 1, :])
    n2, n3 = unpack(high[:BLK, :], high[BLK : BLK + 1, :])
    m1 = n1 + SHIFT * n0
    m2 = n2 + SHIFT * n1
    m3 = n3 + SHIFT * n2
    inverse = invert(m1)
    both = mmh(inverse, jnp.concatenate([m2, n0], 1))
    across = mmh(m2, both)
    schur = m3 - across[:, :BLK]
    y1 = mmh(invert(schur), n1 - across[:, BLK:])
    y0 = both[:, BLK:] - mmh(both[:, :BLK], y1)
    out[:BLK, :] = y0
    out[BLK:, :] = y1


def gather_kernel(irow, wide_h, wide_l, inc, out_h, out_l):
    for u in range(inc.shape[0]):
        at = block_at(irow[u])
        value = backward(inc[u], jnp.concatenate([wide_h[at, :], wide_l[at, :]], 0))
        high, low = split(value)
        out_h[u * BLK : (u + 1) * BLK, :] = high
        out_l[u * BLK : (u + 1) * BLK, :] = low


def combine(left_h, left_l, coef):
    high, low = split(coef)
    return mm(left_h, high) + (mm(left_h, low) + mm(left_l, high))


def scatter_kernel(iblk, core, left_h, left_l, coef, keep, give):
    keep[...] = jnp.zeros(keep.shape, F32)
    give[...] = jnp.zeros(give.shape, F32)
    weights = coef[...]
    for g in range(left_h.shape[0] // (GROUP * BLK)):
        at = slice(g * GROUP * BLK, (g + 1) * GROUP * BLK)
        product = combine(left_h[at, :], left_l[at, :], weights)
        for k in range(GROUP):
            value = product[k * BLK : (k + 1) * BLK, :]
            block = iblk[g * GROUP + k]
            owner = block // SRCB_DEV
            to = owner // 2 * SRCB_DEV + block % SRCB_DEV
            mine = owner % 2 == core[0]

            @pl.when(mine)
            def _():
                keep[to] += value

            @pl.when(jnp.logical_not(mine))
            def _():
                give[to] += value


def third_kernel(left_h, left_l, coef, sol):
    weights = coef[...]
    step = GROUP * BLK
    for g in range(sol.shape[0] // step):
        at = slice(g * step, (g + 1) * step)
        sol[at, :] = combine(left_h[at, :], left_l[at, :], weights)


def call(kernel, n_scalar, n_far, n_vector, outs, scratch=(), mib=16):
    vmem = pl.BlockSpec(memory_space=pltpu.VMEM)
    smem = pl.BlockSpec(memory_space=pltpu.SMEM)
    far = pl.BlockSpec(memory_space=pltpu.HBM)
    return pl.pallas_call(
        kernel,
        in_specs=[smem] * n_scalar + [far] * n_far + [vmem] * n_vector,
        out_specs=[vmem] * len(outs),
        out_shape=[jax.ShapeDtypeStruct(shape, (list(kind) or [F32])[0]) for shape, *kind in outs],
        scratch_shapes=list(scratch),
        compiler_params=pltpu.CompilerParams(vmem_limit_bytes=mib * 1024 * 1024),
    )


def body(
    sides, rhs, diagonal, tile_values, tile_rows, tile_offsets, tile_count, node_count,
    inc_values, inc_rows, inc_blocks,
):
    nx, ny = sides
    nodes, width = rhs.shape
    rowb = nodes // BLK
    head = HB * BLK
    count = 2 * nx * ny
    lead_half = nx * ny * SRCB_DEV
    core = (lax.axis_index("mesh") % 2).astype(jnp.int32)[None]
    diag = diagonal.reshape(rowb, BLK)

    def place(x, y, c):
        return (x % nx * ny + y % ny) * 2 + c

    def moved(value, dx, dy):
        return lax.ppermute(value, "mesh", [
            (place(x, y, c), place(x + dx, y + dy, c))
            for x in range(nx) for y in range(ny) for c in range(2)
        ])

    def swap(value):
        return lax.ppermute(value, "mesh", [(i, i ^ 1) for i in range(count)])

    stay = functools.partial(pltpu.with_memory_space_constraint, memory_space=pltpu.HBM)
    slots = tile_values.shape[0]
    index = pltpu.SMEM((slots,), jnp.int32)
    lines = pltpu.VMEM((rowb, BLK), F32)
    tiles = pltpu.VMEM(tile_values.shape, BF16)
    acc = pltpu.VMEM((rowb + 1, BLK, BLK), F32)
    pieces = pltpu.VMEM((rowb + HB, 2 * BLK, BLK), BF16)
    chosen = index
    tile_args = (tile_count, node_count, *map(stay, (tile_rows, tile_offsets, rhs, diag, tile_values)))
    held = [index, index, pltpu.VMEM((nodes, width), F32), lines, tiles]
    behind, to_chip, to_next = call(
        edge_kernel, 3, 5, 0,
        [((head, width),), ((2 * head + 8, width),), ((2 * head + 8, width),)],
        [
            pltpu.VMEM((2 * head + 8, width), F32), pltpu.VMEM((2 * HB + 1, BLK, BLK), F32),
            pieces, chosen, *held, pltpu.SemaphoreType.DMA((6,)),
        ],
    )(tile_count, node_count, core, *tile_args[2:])
    odd = range(1, count - 1, 2)
    from_next = lax.ppermute(to_next, "mesh", [(i, i + 1) for i in odd] + [(i + 1, i) for i in odd])
    from_chip = swap(to_chip)
    field, part = call(
        first_kernel, 2, 5, 0,
        [((nodes, width),), ((nodes, width),)],
        [acc, pieces, *held, pltpu.SemaphoreType.DMA((5,))],
    )(*tile_args)
    wide_h, wide_l, keep, give = call(
        second_kernel, 3, 4, 5,
        [((nodes, 2 * BLK), BF16), ((nodes, 2 * BLK), BF16), ((BLK + 8, BLK),), ((BLK + 8, BLK),)],
        [
            acc, pieces, pltpu.VMEM((nodes, 2 * BLK), BF16),
            chosen, index, index, lines, tiles, pltpu.SemaphoreType.DMA((4,)),
        ],
    )(tile_count, node_count, core, *map(stay, (tile_rows, tile_offsets, diag, tile_values)),
      field, part, behind, from_chip, from_next)
    total = keep + swap(give)
    total = total + functools.reduce(jnp.add, [moved(total, d, 0) for d in range(1, nx)])
    total = total + functools.reduce(jnp.add, [moved(total, 0, d) for d in range(1, ny)])
    other = swap(total)
    rows = inc_values.shape[0] * BLK
    gather_h, gather_l = call(
        gather_kernel, 1, 0, 3, [((rows, 2 * BLK), BF16), ((rows, 2 * BLK), BF16)]
    )(inc_rows, wide_h, wide_l, inc_values)
    (coef,) = call(solve_kernel, 1, 0, 2, [((2 * BLK, BLK),)])(core, total, other)
    keep, give = call(scatter_kernel, 2, 0, 3, [((lead_half, BLK, BLK),)] * 2)(
        inc_blocks, core, gather_h, gather_l, coef
    )
    other = swap(give)
    (solution,) = call(third_kernel, 0, 0, 3, [((nodes, width),)])(wide_h, wide_l, coef)
    half = (keep + other).reshape(nx * ny, SRCB_DEV * BLK, width)
    groups = [[2 * i + c for i in range(nx * ny)] for c in range(2)]
    got = lax.all_to_all(
        half, "mesh", split_axis=0, concat_axis=0, tiled=True, axis_index_groups=groups
    )
    lead = lax.all_to_all(got.sum(0), "elec", split_axis=0, concat_axis=1, tiled=True)
    return solution, lead


def solution(mesh):
    placed = (
        P("mesh", "elec"),
        P("mesh"),
        P("mesh", None, None),
        P("mesh"),
        P("mesh"),
        P("mesh"),
        P("mesh"),
        P("mesh", None, None),
        P("mesh"),
        P("mesh"),
    )

    def whole(*args):
        return body((4, 4), *args)

    return jax.shard_map(
        whole,
        mesh=mesh,
        in_specs=placed,
        out_specs=(P("mesh", "elec"), P(("mesh", "elec"), None)),
        check_vma=False,
    )
```

```python
import functools

import jax
import jax.numpy as jnp
from jax import lax
from jax.experimental import pallas as pl
from jax.experimental.pallas import tpu as pltpu
from jax.sharding import PartitionSpec as P


HB = 2
SRCB_DEV = 2
BLK = 128
SHIFT = 2.0
F32 = jnp.float32
BF16 = jnp.bfloat16
GROUP = 8
TILE_GROUP = 16


def mm(left, right, dims=((1,), (0,))):
    return lax.dot_general(left, right, (dims, ((), ())), preferred_element_type=F32)


def split(value):
    high = value.astype(BF16)
    return high, (value - high.astype(F32)).astype(BF16)


def rows_of(block):
    return block * BLK + lax.broadcasted_iota(jnp.int32, (BLK, BLK), 0)


def column(line):
    return jnp.transpose(jnp.broadcast_to(line, (BLK, BLK)))


def grouped(count, one, size=GROUP):
    def group(g, carry):
        for add in [one(g * size + k, g * size + k < count) for k in range(size)]:
            for target, index, value in add:
                target[index] += value
        return carry

    lax.fori_loop(0, (count + size - 1) // size, group, 0)


def chosen_loop(count, trow, toff, chosen, wanted, one):
    def scan(t, n):
        chosen[n] = t
        r = trow[t]
        return n + wanted(r, r + toff[t]).astype(jnp.int32)

    n = lax.fori_loop(0, count, scan, 0)
    grouped(n, lambda k, live: one(chosen[jnp.minimum(k, n - 1)], live))


def block_loop(first, last, one):
    steps = (last - first) // GROUP

    def group(g, carry):
        for k in range(GROUP):
            one(first + g * GROUP + k)
        return carry

    lax.fori_loop(0, steps, group, 0)
    for b in range(first + steps * GROUP, last):
        one(b)


def block_at(b):
    return pl.ds(pl.multiple_of(b * BLK, BLK), BLK)


def halves(pieces, b, value):
    high, low = split(value)
    pieces[b, :BLK, :] = high
    pieces[b, BLK:, :] = low
    return high, low


def forward(tile, piece):
    return mm(jnp.concatenate([tile, tile], 1), piece)


def backward(tile, piece):
    flipped = jnp.transpose(tile)
    return mm(jnp.concatenate([flipped, flipped], 1), piece)


def fetch(pairs, sems):
    copies = [
        pltpu.make_async_copy(source, target, sems.at[i])
        for i, (source, target) in enumerate(pairs)
    ]
    for copy in copies:
        copy.start()
    return copies


def edge_kernel(
    tcount, ncount, core, trow_far, toff_far, rhs_far, diag_far, tiles_far,
    behind, to_chip, to_next, ahead, acc, pieces, chosen, trow, toff, rhs, diag, tiles, sems,
):
    head = HB * BLK
    nodes = rhs_far.shape[0]
    rowb = nodes // BLK
    low, high = slice(0, 2 * head), slice(nodes - head, nodes)
    get_low, get_high, get_diag, get_row, get_off, get_tiles = fetch(
        [
            (rhs_far.at[low], rhs.at[low]), (rhs_far.at[high], rhs.at[high]), (diag_far, diag),
            (trow_far, trow), (toff_far, toff), (tiles_far, tiles),
        ],
        sems,
    )
    live = ncount[0]
    spare = 2 * HB
    for copy in (get_low, get_high, get_diag):
        copy.wait()
    for b in [*range(2 * HB), *range(rowb - HB, rowb)]:
        value = jnp.where(rows_of(b) < live, rhs[b * BLK : (b + 1) * BLK, :], 0.0)
        halves(pieces, b, value)
        if b < HB:
            ahead[b * BLK : (b + 1) * BLK, :] = value
            acc[b] = (column(diag[b : b + 1, :]) - SHIFT) * value
    for b in range(HB, 2 * HB):
        acc[b] = jnp.zeros((BLK, BLK), F32)
    for copy in (get_row, get_off, get_tiles):
        copy.wait()

    def one(t, on):
        r = trow[t]
        c = r + toff[t]
        tile = tiles[t]
        inner = jnp.minimum(c, rowb - 1)
        to_row = jnp.where(on & (r < HB), r, spare)
        to_col = jnp.where(c >= rowb, c - rowb + HB, jnp.where(c < HB, c, spare))
        return (
            (acc, to_row, forward(tile, pieces[inner])),
            (acc, jnp.where(on, to_col, spare), backward(tile, pieces[r])),
        )

    chosen_loop(tcount[0], trow, toff, chosen, lambda r, c: (r < HB) | (c >= rowb), one)
    for b in range(HB):
        at = slice(head + b * BLK, head + (b + 1) * BLK)
        ahead[at, :] = jnp.where(rows_of(b) < live, acc[b], 0.0)
        behind[b * BLK : (b + 1) * BLK, :] = acc[HB + b]
    ahead[2 * head :, :] = jnp.full((8, BLK), live.astype(F32))

    def place(lower, upper):
        lower[...] = ahead[...]
        upper[:head, :] = behind[...]
        upper[head:, :] = jnp.zeros((head + 8, BLK), F32)

    @pl.when(core[0] == 0)
    def _():
        place(to_next, to_chip)

    @pl.when(core[0] != 0)
    def _():
        place(to_chip, to_next)


def first_kernel(
    tcount, ncount, trow_far, toff_far, rhs_far, diag_far, tiles_far,
    field, part, acc, pieces, trow, toff, rhs, diag, tiles, sems,
):
    get_rhs, get_diag, get_row, get_off, get_tiles = fetch(
        [(rhs_far, rhs), (diag_far, diag), (trow_far, trow), (toff_far, toff), (tiles_far, tiles)],
        sems,
    )
    get_rhs.wait()
    get_diag.wait()
    rowb = rhs.shape[0] // BLK
    live = ncount[0]
    spare = rowb

    def prepare(b):
        value = jnp.where(rows_of(b) < live, rhs[block_at(b), :], 0.0)
        field[block_at(b), :] = value
        halves(pieces, b, value)
        acc[b] = (column(diag[pl.ds(b, 1), :]) - SHIFT) * value

    block_loop(0, rowb, prepare)
    for copy in (get_row, get_off, get_tiles):
        copy.wait()

    def one(t, on):
        r = trow[t]
        c = r + toff[t]
        tile = tiles[t]
        inside = on & (c < rowb)
        return (
            (acc, jnp.where(inside, r, spare), forward(tile, pieces[jnp.minimum(c, rowb - 1)])),
            (acc, jnp.where(inside, c, spare), backward(tile, pieces[r])),
        )

    grouped(tcount[0], one, TILE_GROUP)

    def finish(b):
        part[block_at(b), :] = jnp.where(rows_of(b) < live, acc[b], 0.0)

    block_loop(0, rowb, finish)


def pack(first, second):
    i = lax.broadcasted_iota(jnp.int32, (BLK, BLK), 0)
    j = lax.broadcasted_iota(jnp.int32, (BLK, BLK), 1)
    line = jnp.sum(jnp.where(i == j, second, 0.0), 0, keepdims=True)
    return jnp.where(i <= j, first, second), line


def unpack(packed, line):
    i = lax.broadcasted_iota(jnp.int32, (BLK, BLK), 0)
    j = lax.broadcasted_iota(jnp.int32, (BLK, BLK), 1)
    flipped = jnp.transpose(packed)
    first = jnp.where(i <= j, packed, flipped)
    second = jnp.where(i > j, packed, flipped)
    return first, jnp.where(i == j, jnp.broadcast_to(line, (BLK, BLK)), second)


def second_kernel(
    tcount, ncount, core,
    trow_far, toff_far, diag_far, tiles_far, field, part, behind, from_chip, from_next,
    wide_h, wide_l, keep, give, acc, pieces, wide_u, chosen, trow, toff, diag, tiles, sems,
):
    get_row, get_off, get_diag, get_tiles = fetch(
        [(trow_far, trow), (toff_far, toff), (diag_far, diag), (tiles_far, tiles)], sems
    )
    rowb = field.shape[0] // BLK
    live = ncount[0]
    count = tcount[0]
    head = HB * BLK
    edge = rowb - HB
    spare = rowb
    even = core[0] == 0
    from_ahead = jnp.where(even, from_chip[...], from_next[...])
    from_behind = jnp.where(even, from_next[:head, :], from_chip[:head, :])

    for b in range(HB):
        halves(pieces, rowb + b, from_ahead[b * BLK : (b + 1) * BLK, :])
        acc[edge + b] = jnp.zeros((BLK, BLK), F32)

    for copy in (get_row, get_off, get_diag, get_tiles):
        copy.wait()

    def reach(t, on):
        r = trow[t]
        value = forward(tiles[t], pieces[r + toff[t]])
        return ((acc, jnp.where(on, r, spare), value),)

    chosen_loop(count, trow, toff, chosen, lambda r, c: c >= rowb, reach)

    count_ahead = from_ahead[2 * head : 2 * head + 1, :]
    for b in range(HB):
        at = slice(b * BLK, (b + 1) * BLK)
        row = rows_of(b).astype(F32)
        value = from_ahead[head + b * BLK : head + (b + 1) * BLK, :]
        halves(pieces, rowb + b, value + jnp.where(row < count_ahead, behind[at, :], 0.0))

    def settle(b, extra=None):
        at = block_at(b)
        value = part[at, :]
        if extra is not None:
            value = value + jnp.where(rows_of(b) < live, extra, 0.0)
        high, low = halves(pieces, b, value)
        wide_h[at, BLK:] = high
        wide_l[at, BLK:] = low
        high, low = split(field[at, :])
        wide_h[at, :BLK] = high
        wide_l[at, :BLK] = low
        acc[b] = (0.5 * (column(diag[pl.ds(b, 1), :]) - SHIFT)) * value

    for b in range(HB):
        settle(b, from_behind[b * BLK : (b + 1) * BLK, :])
    for b in range(edge, rowb):
        settle(b, acc[b])
    block_loop(HB, edge, settle)

    def one(t, on):
        r = trow[t]
        value = forward(tiles[t], pieces[r + toff[t]])
        return ((acc, jnp.where(on, r, spare), value),)

    grouped(count, one, TILE_GROUP)

    def widen(b):
        high, low = split(acc[b])
        wide_u[block_at(b), :BLK] = high
        wide_u[block_at(b), BLK:] = low

    block_loop(0, rowb, widen)

    first = ((0,), (0,))
    straight = mm(wide_h[...], wide_h[...], first)
    cross = mm(wide_h[...], wide_l[...], first)
    n0 = straight[:BLK, :BLK] + cross[:BLK, :BLK] + jnp.transpose(cross[:BLK, :BLK])
    n1 = straight[:BLK, BLK:] + cross[:BLK, BLK:] + jnp.transpose(cross[BLK:, :BLK])
    n2 = straight[BLK:, BLK:] + cross[BLK:, BLK:] + jnp.transpose(cross[BLK:, BLK:])
    both = mm(wide_h[:, BLK:], wide_u[...], first)
    half = both[:, :BLK] + both[:, BLK:] + mm(wide_l[:, BLK:], wide_u[:, :BLK], first)
    n3 = half + jnp.transpose(half)
    n1 = 0.5 * (n1 + jnp.transpose(n1))
    low_packed, low_line = pack(n0, n1)
    high_packed, high_line = pack(n2, n3)

    def place(low_ref, high_ref):
        low_ref[:BLK, :] = low_packed
        low_ref[BLK:, :] = jnp.broadcast_to(low_line, (8, BLK))
        high_ref[:BLK, :] = high_packed
        high_ref[BLK:, :] = jnp.broadcast_to(high_line, (8, BLK))

    @pl.when(core[0] == 0)
    def _():
        place(keep, give)

    @pl.when(core[0] != 0)
    def _():
        place(give, keep)


def pivot_block(columns):
    n = len(columns)
    sub = lax.broadcasted_iota(jnp.int32, columns[0].shape, 0)
    for p in range(n):
        here = sub == p
        row = [jnp.broadcast_to(value[p : p + 1, :], value.shape) for value in columns]
        scale = pl.reciprocal(row[p])
        factor = jnp.where(here, -scale, columns[p] * scale)
        columns = [
            factor if j == p else jnp.where(here, 0.0, columns[j]) - factor * row[j]
            for j in range(n)
        ]
    return columns


def thirds(value):
    high = value.astype(BF16).astype(F32)
    rest = value - high
    middle = rest.astype(BF16).astype(F32)
    return high, middle, rest - middle


def square(left, right):
    lh, lm, ll = (part.astype(BF16) for part in thirds(left))
    rh, rm, rl = (part.astype(BF16) for part in thirds(right))
    small = mm(jnp.concatenate([lm, ll], 1), jnp.concatenate([rm, rh], 0))
    middle = mm(jnp.concatenate([lh, lm], 1), jnp.concatenate([rm, rh], 0))
    return mm(jnp.concatenate([lh, lh], 1), jnp.concatenate([rh, rl], 0)) + (middle + small)


def stacked(left, right):
    lh, lm, ll = thirds(left)
    rh, rm, rl = thirds(right)
    lefts = jnp.concatenate([lh, lh, lh, lm, lm, ll], 0).astype(BF16)
    rights = jnp.concatenate([rh, rm, rl, rh, rm, rh], 0).astype(BF16)
    return mm(lefts, rights, ((0,), (0,)))


def invert(matrix):
    n = matrix.shape[0]
    step = 8
    lane = lax.broadcasted_iota(jnp.int32, (step, n), 1)
    panel = matrix[:step, :]
    for k in range(n // step):
        base = k * step
        inside = (lane >= base) & (lane < base + step)
        columns = [
            jnp.broadcast_to(panel[:, base + j : base + j + 1], (step, n)) for j in range(step)
        ]
        columns = pivot_block(columns)
        rows = None
        unit = columns[0]
        for j in range(step):
            term = columns[j] * panel[j : j + 1, :]
            rows = term if rows is None else rows + term
            unit = jnp.where(lane == base + j, columns[j], unit)
        rows = jnp.where(inside, unit, -rows)
        outer = jnp.where(inside, 0.0, panel)
        cleared = jnp.where(inside[:1, :], 0.0, matrix)
        if k + 1 < n // step:
            ahead = matrix[base + step : base + 2 * step, :]
            panel = cleared[base + step : base + 2 * step, :]
            for j in range(step):
                factor = jnp.broadcast_to(ahead[:, base + j : base + j + 1], (step, n))
                panel = panel - factor * rows[j : j + 1, :]
        matrix = cleared - stacked(outer, rows)
        pieces = []
        if base:
            pieces.append(matrix[:base, :])
        pieces.append(rows)
        if base + step < n:
            pieces.append(panel)
        if base + 2 * step < n:
            pieces.append(matrix[base + 2 * step :, :])
        matrix = jnp.concatenate(pieces, 0)
    return -matrix


def solve_kernel(core, mine, other, out):
    first = core[0] == 0
    low = jnp.where(first, mine[...], other[...])
    high = jnp.where(first, other[...], mine[...])
    n0, n1 = unpack(low[:BLK, :], low[BLK : BLK + 1, :])
    n2, n3 = unpack(high[:BLK, :], high[BLK : BLK + 1, :])
    m1 = n1 + SHIFT * n0
    m2 = n2 + SHIFT * n1
    m3 = n3 + SHIFT * n2
    inverse = invert(m1)
    both = square(inverse, jnp.concatenate([m2, n0], 1))
    across = square(m2, both)
    schur = m3 - across[:, :BLK]
    y1 = square(invert(schur), n1 - across[:, BLK:])
    y0 = both[:, BLK:] - square(both[:, :BLK], y1)
    out[:BLK, :] = y0
    out[BLK:, :] = y1


def gather_kernel(irow, wide_h, wide_l, inc, out_h, out_l):
    for u in range(inc.shape[0]):
        at = block_at(irow[u])
        value = backward(inc[u], jnp.concatenate([wide_h[at, :], wide_l[at, :]], 0))
        high, low = split(value)
        out_h[u * BLK : (u + 1) * BLK, :] = high
        out_l[u * BLK : (u + 1) * BLK, :] = low


def combine(left_h, left_l, coef):
    high, low = split(coef)
    return mm(left_h, high) + (mm(left_h, low) + mm(left_l, high))


def scatter(iblk, wanted, out, value_at):
    out[...] = jnp.zeros(out.shape, F32)
    for u in range(iblk.shape[0]):
        block = iblk[u]
        owner = block // SRCB_DEV
        to = owner // 2 * SRCB_DEV + block % SRCB_DEV

        @pl.when(owner % 2 == wanted)
        def _():
            out[to] += value_at(u)


def scatter_kernel(iblk, core, left_h, left_l, coef, give, products):
    weights = coef[...]
    step = GROUP * BLK
    for g in range(products.shape[0] // step):
        at = slice(g * step, (g + 1) * step)
        products[at, :] = combine(left_h[at, :], left_l[at, :], weights)
    scatter(iblk, 1 - core[0], give, lambda u: products[u * BLK : (u + 1) * BLK, :])


def third_kernel(iblk, core, left_h, left_l, coef, products, sol, keep):
    weights = coef[...]
    step = GROUP * BLK
    for g in range(sol.shape[0] // step):
        at = slice(g * step, (g + 1) * step)
        sol[at, :] = combine(left_h[at, :], left_l[at, :], weights)
    scatter(iblk, core[0], keep, lambda u: products[u * BLK : (u + 1) * BLK, :])


def call(kernel, n_scalar, n_far, n_vector, outs, scratch=(), mib=16):
    vmem = pl.BlockSpec(memory_space=pltpu.VMEM)
    smem = pl.BlockSpec(memory_space=pltpu.SMEM)
    far = pl.BlockSpec(memory_space=pltpu.HBM)
    return pl.pallas_call(
        kernel,
        in_specs=[smem] * n_scalar + [far] * n_far + [vmem] * n_vector,
        out_specs=[vmem] * len(outs),
        out_shape=[jax.ShapeDtypeStruct(shape, (list(kind) or [F32])[0]) for shape, *kind in outs],
        scratch_shapes=list(scratch),
        compiler_params=pltpu.CompilerParams(vmem_limit_bytes=mib * 1024 * 1024),
    )


def body(
    sides, rhs, diagonal, tile_values, tile_rows, tile_offsets, tile_count, node_count,
    inc_values, inc_rows, inc_blocks,
):
    nx, ny = sides
    nodes, width = rhs.shape
    rowb = nodes // BLK
    head = HB * BLK
    count = 2 * nx * ny
    lead_half = nx * ny * SRCB_DEV
    core = (lax.axis_index("mesh") % 2).astype(jnp.int32)[None]
    diag = diagonal.reshape(rowb, BLK)

    def place(x, y, c):
        return (x % nx * ny + y % ny) * 2 + c

    def moved(value, dx, dy):
        return lax.ppermute(value, "mesh", [
            (place(x, y, c), place(x + dx, y + dy, c))
            for x in range(nx) for y in range(ny) for c in range(2)
        ])

    def swap(value):
        return lax.ppermute(value, "mesh", [(i, i ^ 1) for i in range(count)])

    stay = functools.partial(pltpu.with_memory_space_constraint, memory_space=pltpu.HBM)
    slots = tile_values.shape[0]
    index = pltpu.SMEM((slots,), jnp.int32)
    lines = pltpu.VMEM((rowb, BLK), F32)
    tiles = pltpu.VMEM(tile_values.shape, BF16)
    acc = pltpu.VMEM((rowb + 1, BLK, BLK), F32)
    pieces = pltpu.VMEM((rowb + HB, 2 * BLK, BLK), BF16)
    chosen = index
    tile_args = (tile_count, node_count, *map(stay, (tile_rows, tile_offsets, rhs, diag, tile_values)))
    held = [index, index, pltpu.VMEM((nodes, width), F32), lines, tiles]
    behind, to_chip, to_next = call(
        edge_kernel, 3, 5, 0,
        [((head, width),), ((2 * head + 8, width),), ((2 * head + 8, width),)],
        [
            pltpu.VMEM((2 * head + 8, width), F32), pltpu.VMEM((2 * HB + 1, BLK, BLK), F32),
            pieces, chosen, *held, pltpu.SemaphoreType.DMA((6,)),
        ],
    )(tile_count, node_count, core, *tile_args[2:])
    odd = range(1, count - 1, 2)
    from_next = lax.ppermute(to_next, "mesh", [(i, i + 1) for i in odd] + [(i + 1, i) for i in odd])
    from_chip = swap(to_chip)
    field, part = call(
        first_kernel, 2, 5, 0,
        [((nodes, width),), ((nodes, width),)],
        [acc, pieces, *held, pltpu.SemaphoreType.DMA((5,))],
    )(*tile_args)
    wide_h, wide_l, keep, give = call(
        second_kernel, 3, 4, 5,
        [((nodes, 2 * BLK), BF16), ((nodes, 2 * BLK), BF16), ((BLK + 8, BLK),), ((BLK + 8, BLK),)],
        [
            acc, pieces, pltpu.VMEM((nodes, 2 * BLK), BF16),
            chosen, index, index, lines, tiles, pltpu.SemaphoreType.DMA((4,)),
        ],
    )(tile_count, node_count, core, *map(stay, (tile_rows, tile_offsets, diag, tile_values)),
      field, part, behind, from_chip, from_next)
    total = keep + swap(give)
    total = total + functools.reduce(jnp.add, [moved(total, d, 0) for d in range(1, nx)])
    total = total + functools.reduce(jnp.add, [moved(total, 0, d) for d in range(1, ny)])
    other = swap(total)
    rows = inc_values.shape[0] * BLK
    gather_h, gather_l = call(
        gather_kernel, 1, 0, 3, [((rows, 2 * BLK), BF16), ((rows, 2 * BLK), BF16)]
    )(inc_rows, wide_h, wide_l, inc_values)
    (coef,) = call(solve_kernel, 1, 0, 2, [((2 * BLK, BLK),)])(core, total, other)
    give, products = call(
        scatter_kernel, 2, 0, 3, [((lead_half, BLK, BLK),), ((rows, BLK),)]
    )(inc_blocks, core, gather_h, gather_l, coef)
    other = swap(give)
    solution, keep = call(
        third_kernel, 2, 0, 4, [((nodes, width),), ((lead_half, BLK, BLK),)]
    )(inc_blocks, core, wide_h, wide_l, coef, products)
    half = (keep + other).reshape(nx * ny, SRCB_DEV * BLK, width)
    groups = [[2 * i + c for i in range(nx * ny)] for c in range(2)]
    got = lax.all_to_all(
        half, "mesh", split_axis=0, concat_axis=0, tiled=True, axis_index_groups=groups
    )
    lead = lax.all_to_all(got.sum(0), "elec", split_axis=0, concat_axis=1, tiled=True)
    return solution, lead


def solution(mesh):
    placed = (
        P("mesh", "elec"),
        P("mesh"),
        P("mesh", None, None),
        P("mesh"),
        P("mesh"),
        P("mesh"),
        P("mesh"),
        P("mesh", None, None),
        P("mesh"),
        P("mesh"),
    )

    def whole(*args):
        return body((4, 4), *args)

    return jax.shard_map(
        whole,
        mesh=mesh,
        in_specs=placed,
        out_specs=(P("mesh", "elec"), P(("mesh", "elec"), None)),
        check_vma=False,
    )
```
